768 devices in a mesh: dp: 192 (over z, y, core), expert: 4 (over x).
Axes of the slice: x: 4, y: 8, z: 12, core: 2. Of those that a mesh axis runs over, the one named last changes fastest.
Arguments:
- tokens: bfloat16 [98304, 2048], P(('dp', 'expert')), may hold values from -6 to 6
- expert_ids: int32 [98304, 2], P(('dp', 'expert')), may hold values from 0 to 3, all different within a row; in each aligned block of 128 rows (0 to 127, 128 to 255, ...) at most 66 rows name the same one
- gate_probs: bfloat16 [98304, 2], P(('dp', 'expert')), may hold values from 0.099609375 to 1
- w_gate: bfloat16 [4, 2048, 768], P('expert'), may hold values from -0.125 to 0.125
- w_up: bfloat16 [4, 2048, 768], P('expert'), may hold values from -0.125 to 0.125
- w_down: bfloat16 [4, 768, 2048], P('expert'), may hold values from -0.21875 to 0.21875
- teacher_queries: bfloat16 [4, 192, 2048], P('expert', 'dp'), may hold values from -6 to 6
- teacher_passages: bfloat16 [4, 384, 2048], P('expert', 'dp'), may hold values from -6 to 6
- positives: int32 [4, 192], P('expert', 'dp'), may hold values from 0 to 383
Outputs:
- moe_out: bfloat16 [98304, 2048], P(('dp', 'expert'))
- token_grad: bfloat16 [98304, 2048], P(('dp', 'expert'))
- gate_grad: float32 [98304, 2], P(('dp', 'expert'))
- query_loss: float32 [4, 192], P('expert', 'dp')
The draws below stay inside these ranges and needn't reach their ends.
Inputs may be any that keep to these rules, and one draw needn't show every extreme that they name: `expert_ids`: each token names 2 different experts of its group; among the 128 tokens of one device no expert is named more than 66 times, a bound that some block reaches.
All inputs are finite; a program needn't handle non-finite values.
Results may differ from the reference program's by a relative error of at most 0.015.
Values may be sent and summed in bfloat16 or wider, within the bound.
No kernel may reach another device: no remote copies, remote signals or barrier semaphores. Data moves between devices by JAX's collectives and lax.ppermute only.
A program may use at most 64 MiB of HBM per device.

```python
import math
import jax
import jax.numpy as jnp
import numpy as np
from jax import lax

D = 2048
FF = 768
TOP = 2
Q_DEV = 1
QLEN = 32
PLEN = 48
EXPERTS = 4
PASS_DEV = 2
TOK_DEV = 128
CAP = 66
TOKENS = 98304
QROWS = 192
PROWS = 384
BATCHES = 4
N_DP = 192
N_EXPERT = 4


def plant(result, stream_key, least, largest):
    place = [jax.random.randint(jax.random.fold_in(stream_key, axis), (), 0, length) for axis, length in enumerate(result.shape)]
    widest = result.shape.index(max(result.shape))
    next_to = place[:widest] + [(place[widest] + 1) % result.shape[widest]] + place[widest + 1:]
    return result.at[tuple(place)].set(least).at[tuple(next_to)].set(largest)


def block_levels(own_key, extent, split, least, top_value):
    level, own = 1.0, jax.random.fold_in(own_key, 6)
    for axis_at, shards_of in split:
        steps = jnp.exp(jax.random.uniform(jax.random.fold_in(own, axis_at), (shards_of,), jnp.float32, least / len(split), top_value / len(split)))
        level = level * jnp.repeat(steps, extent[axis_at] // shards_of).reshape([-1 if axis == axis_at else 1 for axis in range(len(extent))])
    return level


def routed_block(rng, own, number, rows, amount, top, limit, lean):
    order = jax.random.permutation(rng, amount)
    packed, common = shares(amount, rows * top, limit, lean, True), shares(amount, rows * top, limit, lean, False)
    places = jnp.arange(amount)

    def named(sizes, rotation):
        used = int((sizes > 0).sum())
        fixed = max(1, used // 4)
        moved = fixed + (places - fixed + rotation * (used - fixed)) % max(1, amount - fixed)
        return jnp.zeros((amount,), jnp.int32).at[order[jnp.where(places < fixed, places, moved)]].set(jnp.asarray(sizes, jnp.int32))

    sizes = jnp.where(number % 4 == 0, named(packed, number // 4), named(common, number - number // 4 - 1))
    mixed = jax.random.permutation(jax.random.fold_in(own, 3), amount)
    giver, sink = mixed[0:amount // 2 * 2:2], mixed[1:amount // 2 * 2:2]
    slack = jnp.minimum(sizes[giver] - 1, limit - sizes[sink]) // 2
    slack = jnp.where((giver == order[0]) | (sink == order[0]) | (sizes[sink] == 0), 0, jnp.maximum(slack, 0))
    moved = jax.random.randint(jax.random.fold_in(own, 4), (amount // 2,), 0, 1 << 20) % (slack + 1)
    sizes = sizes.at[giver].add(-moved).at[sink].add(moved)
    members = jnp.searchsorted(jnp.cumsum(sizes), jnp.arange(rows * top), side="right").astype(jnp.int32)
    listing = members.reshape(top, rows).T
    listing = listing[jax.random.permutation(jax.random.fold_in(own, 1), rows)]
    rotation = jax.random.randint(jax.random.fold_in(own, 2), (rows, 1), 0, top)
    return jnp.take_along_axis(listing, (jnp.arange(top)[None, :] + rotation) % top, axis=1)


def shares(amount, total, bound, slope, full):
    weights = [(1 << 20) // math.isqrt(rank ** slope) + 1 for rank in range(1, amount + 1)]
    largest = bound if full else min(bound, max(-(-total // amount), total * weights[0] // sum(weights)))
    least = 1 if total - largest >= amount - 1 else 0
    counts, spare = [largest] + [least] * (amount - 1), total - largest - least * (amount - 1)
    while spare > 0:
        candidates = [i for i in range(1, amount) if counts[i] < largest] or [i for i in range(1, amount) if counts[i] < bound]
        whole, remaining = sum([weights[i] for i in candidates]), spare
        for i in candidates:
            addition = min(bound - counts[i], max(1, remaining * weights[i] // whole), spare)
            counts[i] = counts[i] + addition
            spare = spare - addition
    return np.array(counts)


def normal_values(rng, dims, spread, most, split=(), held_as=jnp.bfloat16):
    array = jax.random.normal(rng, dims, jnp.float32) * spread
    if len(split) > 0:
        array = block_levels(rng, dims, split, -0.22, 0.18) * array
    return jnp.clip(array, min=-most, max=most).astype(held_as)


def setup_inputs(seed: int = 0) -> dict:
    seeds = jax.random.split(jax.random.key(seed), 10)
    tokens = normal_values(seeds[0], (TOKENS, D), 1.0, 6.0, ((0, 768),))
    expert_ids_keys = jax.random.split(jax.random.fold_in(seeds[1], 1), TOKENS // TOK_DEV)
    expert_ids_turns = jax.random.permutation(jax.random.fold_in(seeds[1], 3), TOKENS // TOK_DEV)
    expert_ids = jax.vmap(lambda own, number: routed_block(jax.random.fold_in(seeds[1], 2), own, number, TOK_DEV, EXPERTS, TOP, CAP, 2))(expert_ids_keys, expert_ids_turns).reshape((TOKENS, TOP))
    gate_probs = jnp.clip(jnp.exp(math.log(1.0) - 2.306499 * jax.random.uniform(seeds[2], (TOKENS, TOP), jnp.float32) ** block_levels(seeds[2], (TOKENS, TOP), ((0, 768),), -0.2, 0.2)), 0.099609375, 1.0).astype(jnp.bfloat16)
    w_gate = normal_values(seeds[3], (EXPERTS, D, FF), D ** -0.5, 0.125, ((0, 4),))
    w_up = normal_values(seeds[4], (EXPERTS, D, FF), D ** -0.5, 0.125, ((0, 4),))
    w_down = normal_values(seeds[5], (EXPERTS, FF, D), FF ** -0.5, 0.21875, ((0, 4),))
    teacher_queries = normal_values(seeds[6], (BATCHES, QROWS, D), 1.0, 6.0, ((0, 4), (1, 192)))
    teacher_passages = normal_values(seeds[7], (BATCHES, PROWS, D), 1.0, 6.0, ((0, 4), (1, 192)))
    positives = plant(jax.random.randint(seeds[8], (BATCHES, QROWS), 0, PROWS), jax.random.fold_in(seeds[8], 1), 0, PROWS - 1).astype(jnp.int32)
    return dict(tokens=tokens, expert_ids=expert_ids, gate_probs=gate_probs, w_gate=w_gate, w_up=w_up, w_down=w_down, teacher_queries=teacher_queries, teacher_passages=teacher_passages, positives=positives)


student_scale = 50.0
teacher_scale = 80.0
loss_scale = 64.0
norm_eps = 1e-06
highest = lax.Precision.HIGHEST

def silu_slope(pre_gate):
    sigmoid = jax.nn.sigmoid(pre_gate)
    return sigmoid * (1.0 + pre_gate * (1.0 - sigmoid))

def expert_forward(expert_args):
    routed, gate_mat, up_mat, down_mat = expert_args
    routed_f = routed.astype(jnp.float32)
    pre_gate = jnp.dot(routed_f, gate_mat, precision=highest)
    pre_up = jnp.dot(routed_f, up_mat, precision=highest)
    hidden = (jax.nn.silu(pre_gate) * pre_up).astype(jnp.bfloat16)
    return jnp.dot(hidden.astype(jnp.float32), down_mat, precision=highest).astype(jnp.bfloat16)

def expert_apply(expert_args):
    routed, routed_grad, gate_mat, up_mat, down_mat = expert_args
    routed_f = routed.astype(jnp.float32)
    grad_f = routed_grad.astype(jnp.float32)
    pre_gate = jnp.dot(routed_f, gate_mat, precision=highest)
    pre_up = jnp.dot(routed_f, up_mat, precision=highest)
    activation = jax.nn.silu(pre_gate)
    hidden = (activation * pre_up).astype(jnp.bfloat16)
    expert_out = jnp.dot(hidden.astype(jnp.float32), down_mat, precision=highest).astype(jnp.bfloat16)
    hidden_grad = jnp.dot(grad_f, down_mat.T, precision=highest)
    gate_part = (hidden_grad * pre_up * silu_slope(pre_gate)).astype(jnp.bfloat16)
    up_part = (hidden_grad * activation).astype(jnp.bfloat16)
    row_grad = jnp.dot(gate_part.astype(jnp.float32), gate_mat.T, precision=highest)
    row_grad = row_grad + jnp.dot(up_part.astype(jnp.float32), up_mat.T, precision=highest)
    return (expert_out, row_grad.astype(jnp.bfloat16))

def slot_numbers(group_ids):
    flat_ids = group_ids.reshape(-1).astype(jnp.int32)
    per_source = TOK_DEV * TOP
    expert_hits = (flat_ids[:, None] == jnp.arange(EXPERTS, dtype=jnp.int32)[None, :]).astype(jnp.int32)
    blocks = expert_hits.reshape(N_EXPERT, per_source, EXPERTS)
    earlier = (jnp.cumsum(blocks, axis=1) - blocks).reshape(-1, EXPERTS)
    slot_rank = lax.optimization_barrier(jnp.sum(earlier * expert_hits, axis=1))
    source = jnp.arange(flat_ids.shape[0], dtype=jnp.int32) // per_source
    return (flat_ids * (N_EXPERT * CAP) + source * CAP + slot_rank).astype(jnp.int32)

def unit_rows(values):
    as_float = values.astype(jnp.float32)
    inverse = lax.rsqrt(lax.optimization_barrier(jnp.sum(as_float * as_float, axis=-1, keepdims=True)) + norm_eps)
    return (as_float * inverse, inverse)

def unit_back(normed, inverse, grad_normed):
    return inverse * (grad_normed - normed * lax.optimization_barrier(jnp.sum(normed * grad_normed, axis=-1, keepdims=True)))

def batch_pass(batch_args):
    query_block, passage_block, teacher_q_block, teacher_p_block, positive_block = batch_args
    query_unit, query_inv = unit_rows(query_block)
    passage_unit, passage_inv = unit_rows(passage_block)
    query_half = query_unit.astype(jnp.bfloat16)
    passage_half = passage_unit.astype(jnp.bfloat16)
    teacher_q_half = unit_rows(teacher_q_block)[0].astype(jnp.bfloat16)
    teacher_p_half = unit_rows(teacher_p_block)[0].astype(jnp.bfloat16)
    student = student_scale * jnp.dot(query_half, passage_half.T, preferred_element_type=jnp.float32)
    teacher = teacher_scale * jnp.dot(teacher_q_half, teacher_p_half.T, preferred_element_type=jnp.float32)
    student_exp = jnp.exp(student)
    teacher_exp = jnp.exp(teacher)
    student_total = lax.optimization_barrier(jnp.sum(student_exp, axis=1))
    teacher_total = lax.optimization_barrier(jnp.sum(teacher_exp, axis=1))
    cross_term = lax.optimization_barrier(jnp.sum(teacher_exp * (teacher - student), axis=1))
    is_positive = positive_block[:, None] == jnp.arange(PROWS, dtype=jnp.int32)[None, :]
    positive_score = lax.optimization_barrier(jnp.sum(jnp.where(is_positive, student, 0.0), axis=1))
    query_loss = 2.0 * jnp.log(student_total) - positive_score + cross_term / teacher_total - jnp.log(teacher_total)
    coeffs = (2.0 * student_exp / student_total[:, None] - teacher_exp / teacher_total[:, None] - is_positive.astype(jnp.float32)).astype(jnp.bfloat16)
    unit_q_grad = student_scale * jnp.dot(coeffs, passage_half, preferred_element_type=jnp.float32)
    unit_p_grad = student_scale * jnp.dot(coeffs.T, query_half, preferred_element_type=jnp.float32)
    return (query_loss, unit_back(query_unit, query_inv, unit_q_grad), unit_back(passage_unit, passage_inv, unit_p_grad))

def reference(tokens, expert_ids, gate_probs, w_gate, w_up, w_down, teacher_queries, teacher_passages, positives):
    gate_full = w_gate.astype(jnp.float32)
    up_full = w_up.astype(jnp.float32)
    down_full = w_down.astype(jnp.float32)
    group_tokens = TOK_DEV * N_EXPERT
    slot_total = EXPERTS * N_EXPERT * CAP

    def forward_group(group_args):
        tok_block, id_block, prob_block = group_args
        slot_index = slot_numbers(id_block)
        token_rep = jnp.repeat(tok_block, TOP, axis=0)
        rows_in = jnp.zeros((slot_total, D), jnp.bfloat16).at[slot_index].set(token_rep)
        expert_out = lax.map(expert_forward, (rows_in.reshape(EXPERTS, N_EXPERT * CAP, D), gate_full, up_full, down_full))
        token_out = expert_out.reshape(slot_total, D)[slot_index].astype(jnp.float32)
        prob_flat = prob_block.reshape(-1, 1).astype(jnp.float32)
        return lax.optimization_barrier(jnp.sum((prob_flat * token_out).reshape(group_tokens, TOP, D), axis=1)).astype(jnp.bfloat16)
    tok_groups = tokens.reshape(N_DP, group_tokens, D)
    id_groups = expert_ids.reshape(N_DP, group_tokens, TOP)
    prob_groups = gate_probs.reshape(N_DP, group_tokens, TOP)
    moe_out = lax.map(forward_group, (tok_groups, id_groups, prob_groups)).reshape(TOKENS, D)
    moe_blocks = moe_out.reshape(N_DP, N_EXPERT, TOK_DEV, D)
    query_tokens = moe_blocks[:, :, :Q_DEV * QLEN].reshape(N_DP, N_EXPERT, Q_DEV, QLEN, D)
    passage_tokens = moe_blocks[:, :, Q_DEV * QLEN:].reshape(N_DP, N_EXPERT, PASS_DEV, PLEN, D)
    pooled_q = lax.optimization_barrier(jnp.mean(query_tokens.astype(jnp.float32), axis=3))
    pooled_p = lax.optimization_barrier(jnp.mean(passage_tokens.astype(jnp.float32), axis=3))
    pooled_q = jnp.transpose(pooled_q, (1, 0, 2, 3)).reshape(BATCHES, QROWS, D)
    pooled_p = jnp.transpose(pooled_p, (1, 0, 2, 3)).reshape(BATCHES, PROWS, D)
    query_loss, query_grad, passage_grad = lax.map(batch_pass, (pooled_q, pooled_p, teacher_queries, teacher_passages, positives))
    q_grad_blocks = jnp.transpose(query_grad.reshape(BATCHES, N_DP, Q_DEV, D), (1, 0, 2, 3))
    p_grad_blocks = jnp.transpose(passage_grad.reshape(BATCHES, N_DP, PASS_DEV, D), (1, 0, 2, 3))

    def backward_group(group_args):
        tok_block, id_block, prob_block, q_grad_block, p_grad_block = group_args
        query_part = jnp.repeat(q_grad_block * (loss_scale / QLEN), QLEN, axis=1)
        passage_part = jnp.repeat(p_grad_block * (loss_scale / PLEN), PLEN, axis=1)
        out_grad = jnp.concatenate([query_part, passage_part], axis=1).reshape(group_tokens, D)
        slot_index = slot_numbers(id_block)
        token_rep = jnp.repeat(tok_block, TOP, axis=0)
        grad_rep = jnp.repeat(out_grad, TOP, axis=0)
        prob_flat = prob_block.reshape(-1, 1).astype(jnp.float32)
        routed_grad = (prob_flat * grad_rep).astype(jnp.bfloat16)
        rows_in = jnp.zeros((slot_total, D), jnp.bfloat16).at[slot_index].set(token_rep)
        grads_in = jnp.zeros((slot_total, D), jnp.bfloat16).at[slot_index].set(routed_grad)
        expert_out, row_grad = lax.map(expert_apply, (rows_in.reshape(EXPERTS, N_EXPERT * CAP, D), grads_in.reshape(EXPERTS, N_EXPERT * CAP, D), gate_full, up_full, down_full))
        token_out = expert_out.reshape(slot_total, D)[slot_index].astype(jnp.float32)
        token_row_grad = row_grad.reshape(slot_total, D)[slot_index].astype(jnp.float32)
        grad_block = lax.optimization_barrier(jnp.sum(token_row_grad.reshape(group_tokens, TOP, D), axis=1)).astype(jnp.bfloat16)
        gate_block = lax.optimization_barrier(jnp.sum(token_out * grad_rep, axis=1)).reshape(group_tokens, TOP)
        return (grad_block, gate_block)
    token_grad, gate_grad = lax.map(backward_group, (tok_groups, id_groups, prob_groups, q_grad_blocks, p_grad_blocks))
    token_grad = token_grad.reshape(TOKENS, D)
    gate_grad = gate_grad.reshape(TOKENS, TOP)
    return (moe_out, token_grad, gate_grad, query_loss)
```

```python
import functools

import jax
import jax.numpy as jnp
import numpy as np
from jax import lax
from jax.experimental import pallas as pl
from jax.experimental.pallas import tpu as pltpu
from jax.sharding import Mesh
from jax.sharding import PartitionSpec as P

QLEN = 32
PLEN = 48
SEGS = 3
CHUNKS = 8
Z_CHIPS = 12

student_scale = 50.0
teacher_scale = 80.0
loss_scale = 64.0
norm_eps = 1e-06

f32 = jnp.float32
bf16 = jnp.bfloat16
exact = lax.Precision.HIGHEST


def iota(shape, axis):
    return lax.broadcasted_iota(jnp.int32, shape, axis)


def dot(left, right, dims=((1,), (0,)), precision=None):
    return lax.dot_general(left, right, (dims, ((), ())), precision=precision, preferred_element_type=f32)


def silu_slope(pre_gate):
    sigmoid = jax.nn.sigmoid(pre_gate)
    return sigmoid * (1.0 + pre_gate * (1.0 - sigmoid))


def segment_mask(rows, count, repeat):
    token = iota((rows, count), 1)
    text = jnp.where(token < QLEN, 0, jnp.where(token < QLEN + PLEN, 1, 2))
    return (text == iota((rows, count), 0) // repeat).astype(f32)


def routing(ids):
    count = ids.shape[1]
    expert = iota((8, count), 0)
    first = expert == ids[0:1, :]
    second = expert == ids[1:2, :]
    hit = jnp.where(first, 1.0, jnp.where(second, 1.0, 0.0))
    before = (iota((count, count), 0) < iota((count, count), 1)).astype(bf16)
    rank = dot(hit.astype(bf16), before)
    return jnp.where(hit > 0.0, rank, -1.0), first, second


def slot_hits(rank, experts, rows):
    count = rank.shape[1]
    slot = iota((rows, count), 0).astype(f32)
    return [(slot == rank[e : e + 1, :]).astype(f32) for e in range(experts)]


def dispatch_kernel(tok_ref, ids_ref, prob_ref, send_ref, *, experts, cap, rows):
    count = tok_ref.shape[0]
    rank, first, second = routing(ids_ref[...])
    probs = prob_ref[...].astype(f32)
    weight = jnp.where(first, probs[0:1, :], jnp.where(second, probs[1:2, :], 0.0))
    wide = slot_hits(rank, experts, 128)
    segs = segment_mask(8, count, 1)
    place = (iota((rows, 8), 0) == cap + iota((rows, 8), 1)).astype(bf16)
    metas = []
    for e in range(experts):
        by_text = (segs * weight[e : e + 1, :]).astype(bf16)
        meta = dot(by_text, wide[e].astype(bf16), ((1,), (1,)))
        metas.append(dot(place, meta.astype(bf16)))
    pick = jnp.concatenate([hits[:rows] for hits in wide], axis=0).astype(bf16)
    width = tok_ref.shape[1]
    send_ref[:, 0:128] = (dot(pick, tok_ref[:, 0:128]) + jnp.concatenate(metas, axis=0)).astype(bf16)
    send_ref[:, 128:width] = dot(pick, tok_ref[:, 128:width]).astype(bf16)


def unit_block(values):
    inverse = lax.rsqrt(jnp.sum(values * values, keepdims=True) + norm_eps)
    return values * inverse, inverse


def to_chunks(row, size):
    which = iota((CHUNKS, size), 0)
    out = jnp.zeros((CHUNKS, size), f32)
    for j in range(CHUNKS):
        out = jnp.where(which == j, row[:, j * size : (j + 1) * size], out)
    return out


def combine_kernel(
    ret_ref, ids_ref, prob_ref, tq_ref, tp_ref, pos_ref, moe_ref, unit_ref, inv_ref, qs_ref, ps_ref, *, experts, rows
):
    count = ids_ref.shape[1]
    width = ret_ref.shape[1]
    size = width // CHUNKS
    rank, first, second = routing(ids_ref[...])
    probs = prob_ref[...].astype(f32)
    weight = jnp.where(first, probs[0:1, :], jnp.where(second, probs[1:2, :], 0.0))
    hits = slot_hits(rank, experts, rows)
    mix = jnp.concatenate([hits[e] * weight[e : e + 1, :] for e in range(experts)], axis=0).astype(bf16)
    moe = dot(mix, ret_ref[...], ((0,), (0,))).astype(bf16)
    moe_ref[...] = moe
    member = segment_mask(SEGS * CHUNKS, count, CHUNKS).astype(bf16)
    chunk = iota((SEGS * CHUNKS, size), 0) % CHUNKS
    pooled = jnp.zeros((SEGS * CHUNKS, size), f32)
    for j in range(CHUNKS):
        pooled = jnp.where(chunk == j, dot(member, moe[:, j * size : (j + 1) * size]), pooled)
    query, query_inv = unit_block(pooled[0:8] * (1.0 / QLEN))
    pass_a, pass_a_inv = unit_block(pooled[8:16] * (1.0 / PLEN))
    pass_b, pass_b_inv = unit_block(pooled[16:24] * (1.0 / PLEN))
    unit_ref[...] = jnp.concatenate([query, pass_a, pass_b], axis=0)
    inv_ref[...] = jnp.concatenate(
        [jnp.broadcast_to(inverse, (8, 128)) for inverse in (query_inv, pass_a_inv, pass_b_inv)], axis=0
    )
    teach_q = unit_block(to_chunks(tq_ref[...].astype(f32), size))[0]
    teach_p = tp_ref[...].astype(f32)
    teach_a = unit_block(to_chunks(teach_p[0:1], size))[0]
    teach_b = unit_block(to_chunks(teach_p[1:2], size))[0]
    pos = pos_ref[0, 0]
    lane = iota((8, size), 1)
    marks = jnp.where(lane == 0, (pos >> 4).astype(f32), jnp.where(lane == 1, (pos & 15).astype(f32), 0.0))
    queries = jnp.concatenate([query, teach_q, marks], axis=0).astype(bf16)
    passages = jnp.concatenate([pass_a, pass_b, teach_a, teach_b], axis=0).astype(bf16)
    for peer in range(qs_ref.shape[0]):
        qs_ref[peer] = queries
    for peer in range(ps_ref.shape[0]):
        ps_ref[peer] = passages


def passage_of(col):
    return (col // 32) * 2 + (col % 16) // 8


def score_kernel(q_ref, p_ref, me_ref, sums_ref, saved_ref, *, peers):
    q_rows = q_ref.shape[0]
    p_rows = p_ref.shape[0]
    valid_count = p_rows // 16
    queries = q_ref[...]
    products = dot(queries, p_ref[...], ((1,), (1,)))
    row = iota((q_rows, p_rows), 0)
    col = iota((q_rows, p_rows), 1)
    kind = row % 24 // 8
    wanted = jnp.where(col % 32 < 16, 0, 1)
    products = jnp.where((kind == wanted) & (row % 8 == col % 8), products, 0.0)
    pick_row = iota((2 * peers, q_rows), 0)
    pick_col = iota((2 * peers, q_rows), 1)
    pick = ((pick_col // 24 == pick_row % peers) & (pick_col % 24 // 8 == pick_row // peers)).astype(f32)
    join = (passage_of(iota((p_rows, 128), 0)) == iota((p_rows, 128), 1)).astype(f32)
    scores = dot(dot(pick, products, precision=exact), join, precision=exact)
    student = student_scale * scores[0:peers]
    teacher = teacher_scale * scores[peers : 2 * peers]
    mark_pick = (iota((peers, q_rows), 1) == 24 * iota((peers, q_rows), 0) + 16).astype(bf16)
    marks = dot(mark_pick, queries)
    pos = (16.0 * marks[:, 0:1] + marks[:, 1:2]).astype(jnp.int32)
    lane = iota((peers, 128), 1)
    me = me_ref[0, 0]
    number = (lane // 2) * (2 * peers) + lane % 2 + 2 * me
    valid = lane < valid_count
    is_pos = jnp.where(valid & (number == pos), 1.0, 0.0)
    student_exp = jnp.where(valid, jnp.exp(student), 0.0)
    teacher_exp = jnp.where(valid, jnp.exp(teacher), 0.0)
    total = lambda values: jnp.sum(values, axis=1, keepdims=True)
    sums = jnp.where(
        lane == 0,
        total(student_exp),
        jnp.where(
            lane == 1,
            total(teacher_exp),
            jnp.where(
                lane == 2, total(teacher_exp * (teacher - student)), jnp.where(lane == 3, total(is_pos * student), 0.0)
            ),
        ),
    )
    for peer in range(peers):
        sums_ref[peer] = sums
    saved_ref[0] = student_exp
    saved_ref[1] = teacher_exp
    saved_ref[2] = is_pos


def coeff_kernel(sums_ref, saved_ref, q_ref, p_ref, me_ref, dq_ref, dp_ref, loss_ref, *, peers):
    q_rows = q_ref.shape[0]
    p_rows = p_ref.shape[0]
    sums = sums_ref[0]
    for peer in range(1, peers):
        sums = sums + sums_ref[peer]
    student_total = sums[:, 0:1]
    teacher_total = sums[:, 1:2]
    loss = 2.0 * jnp.log(student_total) - sums[:, 3:4] + sums[:, 2:3] / teacher_total - jnp.log(teacher_total)
    mine = iota((peers, 128), 0) == me_ref[0, 0]
    loss_ref[...] = jnp.sum(jnp.where(mine, loss, 0.0), axis=0, keepdims=True)
    coeffs = (2.0 * saved_ref[0] / student_total - saved_ref[1] / teacher_total - saved_ref[2]).astype(bf16)
    rows = peers * CHUNKS
    spread = (iota((rows, peers), 0) // CHUNKS == iota((rows, peers), 1)).astype(bf16)
    join = (iota((128, p_rows), 0) == passage_of(iota((128, p_rows), 1))).astype(bf16)
    by_query = dot(dot(spread, coeffs).astype(bf16), join)
    row = iota((rows, p_rows), 0)
    col = iota((rows, p_rows), 1)
    by_query = jnp.where((col % 32 < 16) & (row % 8 == col % 8), by_query, 0.0).astype(bf16)
    dq_ref[...] = student_scale * dot(by_query, p_ref[...])
    rows = p_rows // 2
    spread = (iota((rows, 128), 0) // CHUNKS == iota((rows, 128), 1)).astype(bf16)
    join = (iota((peers, q_rows), 0) == iota((peers, q_rows), 1) // 24).astype(bf16)
    by_passage = dot(dot(spread, coeffs, ((1,), (1,))).astype(bf16), join)
    row = iota((rows, q_rows), 0)
    col = iota((rows, q_rows), 1)
    by_passage = jnp.where((col % 24 < 8) & (row % 8 == col % 8), by_passage, 0.0).astype(bf16)
    dp_ref[...] = student_scale * dot(by_passage, q_ref[...])


def grad_kernel(dq_ref, dp_ref, unit_ref, inv_ref, grad_ref, sent_ref):
    query = dq_ref[0]
    for peer in range(1, dq_ref.shape[0]):
        query = query + dq_ref[peer]
    passage = dp_ref[0]
    for peer in range(1, dp_ref.shape[0]):
        passage = passage + dp_ref[peer]
    parts = []
    for s, (unit_grad, scale) in enumerate(
        ((query, loss_scale / QLEN), (passage[0:8], loss_scale / PLEN), (passage[8:16], loss_scale / PLEN))
    ):
        unit = unit_ref[8 * s : 8 * s + 8, :]
        inverse = inv_ref[8 * s : 8 * s + 8, 0:1]
        along = jnp.sum(unit * unit_grad, keepdims=True)
        parts.append(scale * (inverse * (unit_grad - unit * along)))
    grad = jnp.concatenate(parts, axis=0)
    grad_ref[...] = grad
    for peer in range(sent_ref.shape[0]):
        sent_ref[peer] = grad


def gate_grad_kernel(ret_ref, ids_ref, grad_ref, out_ref, *, experts, rows):
    count = ids_ref.shape[1]
    size = ret_ref.shape[1] // CHUNKS
    slots = ret_ref.shape[0]
    rank, first, second = routing(ids_ref[...])
    grad = grad_ref[...]
    high = grad.astype(bf16)
    low = (grad - high.astype(f32)).astype(bf16)
    both = jnp.concatenate([high.astype(f32), low.astype(f32)], axis=0).astype(bf16)
    n = 2 * SEGS * CHUNKS
    chunk = iota((n, slots), 0) % CHUNKS
    acc = jnp.zeros((n, slots), f32)
    for j in range(CHUNKS):
        part = dot(both, ret_ref[:, j * size : (j + 1) * size], ((1,), (1,)))
        acc = jnp.where(chunk == j, part, acc)
    gather = (iota((8, n), 1) // CHUNKS % SEGS == iota((8, n), 0)).astype(f32)
    by_slot = dot(gather, acc, precision=exact)
    hits = slot_hits(rank, experts, rows)
    texts = segment_mask(8, count, 1)
    results = []
    for named in (first, second):
        named = jnp.where(named, 1.0, 0.0)
        pick = jnp.concatenate([hits[e] * named[e : e + 1, :] for e in range(experts)], axis=0)
        results.append(jnp.sum(texts * dot(by_slot, pick, precision=exact), axis=0, keepdims=True))
    out_ref[...] = jnp.where(iota((2, count), 0) == 0, results[0], results[1])


def token_grad_kernel(back_ref, ids_ref, out_ref, *, experts, rows):
    rank, _, _ = routing(ids_ref[...])
    pick = jnp.concatenate(slot_hits(rank, experts, rows), axis=0).astype(bf16)
    out_ref[...] = dot(pick, back_ref[...], ((0,), (0,))).astype(bf16)


def vmem(count):
    return [pl.BlockSpec(memory_space=pltpu.VMEM)] * count


SMEM = pl.BlockSpec(memory_space=pltpu.SMEM)


def shape_of(*dims, dtype=f32):
    return jax.ShapeDtypeStruct(dims, dtype)


def exchange(values, axis):
    return lax.all_to_all(values, axis, split_axis=0, concat_axis=0, tiled=True)


def shards(
    tokens,
    expert_ids,
    gate_probs,
    w_gate,
    w_up,
    w_down,
    teacher_queries,
    teacher_passages,
    positives,
):
    experts = lax.axis_size("expert")
    peers = lax.axis_size("yc")
    chips = lax.axis_size("z")
    count, width = tokens.shape
    size = width // CHUNKS
    top = expert_ids.shape[1]
    cap = min(count, (count * top * 33 + 32 * experts - 1) // (32 * experts))
    rows = (cap + SEGS + 7) // 8 * 8
    slots = experts * rows
    ids = expert_ids.T
    probs = gate_probs.T
    me = lax.axis_index("yc").astype(jnp.int32).reshape(1, 1)
    gate_mat = w_gate[0]
    up_mat = w_up[0]
    down_mat = w_down[0]

    sent = pl.pallas_call(
        functools.partial(dispatch_kernel, experts=experts, cap=cap, rows=rows),
        out_shape=shape_of(slots, width, dtype=bf16),
        in_specs=vmem(3),
        out_specs=vmem(1)[0],
        name="dispatch",
    )(tokens, ids, probs)
    arrived = exchange(sent.reshape(experts, rows, width), "expert")
    arrived_rows = arrived.reshape(slots, width)
    pre_gate = jnp.dot(arrived_rows, gate_mat, preferred_element_type=f32)
    pre_up = jnp.dot(arrived_rows, up_mat, preferred_element_type=f32)
    hidden = (jax.nn.silu(pre_gate) * pre_up).astype(bf16)
    expert_out = jnp.dot(hidden, down_mat, preferred_element_type=f32).astype(bf16)
    returned = exchange(expert_out.reshape(experts, rows, width), "expert").reshape(slots, width)

    moe_out, unit, inverse, q_sent, p_sent = pl.pallas_call(
        functools.partial(combine_kernel, experts=experts, rows=rows),
        out_shape=(
            shape_of(count, width, dtype=bf16),
            shape_of(SEGS * CHUNKS, size),
            shape_of(SEGS * CHUNKS, 128),
            shape_of(peers, 24, size, dtype=bf16),
            shape_of(chips, 32, size, dtype=bf16),
        ),
        in_specs=vmem(5) + [SMEM],
        out_specs=tuple(vmem(5)),
        name="combine",
    )(returned, ids, probs, teacher_queries[0], teacher_passages[0], positives)
    q_all = exchange(q_sent, "yc").reshape(peers * 24, size)
    p_all = exchange(p_sent, "z").reshape(chips * 32, size)
    sums_sent, saved = pl.pallas_call(
        functools.partial(score_kernel, peers=peers),
        out_shape=(shape_of(peers, peers, 128), shape_of(3, peers, 128)),
        in_specs=vmem(2) + [SMEM],
        out_specs=tuple(vmem(2)),
        name="score",
    )(q_all, p_all, me)
    sums = exchange(sums_sent, "yc")
    dq_sent, dp_sent, loss = pl.pallas_call(
        functools.partial(coeff_kernel, peers=peers),
        out_shape=(shape_of(peers * CHUNKS, size), shape_of(chips * 16, size), shape_of(1, 128)),
        in_specs=vmem(4) + [SMEM],
        out_specs=tuple(vmem(3)),
        name="coeff",
    )(sums, saved, q_all, p_all, me)
    dq = exchange(dq_sent.reshape(peers, CHUNKS, size), "yc")
    dp = exchange(dp_sent.reshape(chips, 2 * CHUNKS, size), "z")
    grad, grad_sent = pl.pallas_call(
        grad_kernel,
        out_shape=(shape_of(SEGS * CHUNKS, size), shape_of(experts, SEGS * CHUNKS, size)),
        in_specs=vmem(4),
        out_specs=tuple(vmem(2)),
        name="text_grad",
    )(dq, dp, unit, inverse)
    grad_all = exchange(grad_sent, "expert").reshape(experts * SEGS, width)

    grad_high = grad_all.astype(bf16)
    grad_low = (grad_all - grad_high.astype(f32)).astype(bf16)
    text_hidden = lax.dot_general(
        jnp.concatenate([grad_high, grad_low], axis=0),
        down_mat,
        (((1,), (1,)), ((), ())),
        preferred_element_type=f32,
    )
    text_hidden = (text_hidden[: experts * SEGS] + text_hidden[experts * SEGS :]).reshape(experts, SEGS, -1)
    share = arrived[:, cap : cap + SEGS, :rows].astype(f32)
    hidden_grad = sum(share[:, s, :, None] * text_hidden[:, s, None, :] for s in range(SEGS)).reshape(slots, -1)
    gate_part = (hidden_grad * pre_up * silu_slope(pre_gate)).astype(bf16)
    up_part = (hidden_grad * jax.nn.silu(pre_gate)).astype(bf16)
    row_grad = (
        dot(gate_part, gate_mat, ((1,), (1,))) + dot(up_part, up_mat, ((1,), (1,)))
    ).astype(bf16)
    back = exchange(row_grad.reshape(experts, rows, width), "expert").reshape(slots, width)
    gate_grad = pl.pallas_call(
        functools.partial(gate_grad_kernel, experts=experts, rows=rows),
        out_shape=shape_of(top, count),
        in_specs=vmem(3),
        out_specs=vmem(1)[0],
        name="gate_grad",
    )(returned, ids, grad)
    token_grad = pl.pallas_call(
        functools.partial(token_grad_kernel, experts=experts, rows=rows),
        out_shape=shape_of(count, width, dtype=bf16),
        in_specs=vmem(2),
        out_specs=vmem(1)[0],
        name="token_grad",
    )(back, ids)
    return (moe_out, token_grad, gate_grad.T, loss[:, :1])


def solution(mesh):
    dp, expert = mesh.devices.shape
    chips = Z_CHIPS if dp % Z_CHIPS == 0 else 2
    grid = Mesh(np.asarray(mesh.devices).reshape(chips, dp // chips, expert), ("z", "yc", "expert"))
    every = ("z", "yc", "expert")
    in_specs = (
        P(every, None),
        P(every, None),
        P(every, None),
        P("expert", None, None),
        P("expert", None, None),
        P("expert", None, None),
        P("expert", ("z", "yc"), None),
        P("expert", ("z", "yc"), None),
        P("expert", ("z", "yc")),
    )
    out_specs = (
        P(every, None),
        P(every, None),
        P(every, None),
        P("expert", ("z", "yc")),
    )
    return jax.shard_map(shards, mesh=grid, in_specs=in_specs, out_specs=out_specs, check_vma=False)
```

```python
import functools

import jax
import jax.numpy as jnp
import numpy as np
from jax import lax
from jax.experimental import pallas as pl
from jax.experimental.pallas import tpu as pltpu
from jax.sharding import Mesh
from jax.sharding import PartitionSpec as P

QLEN = 32
PLEN = 48
SEGS = 3
CHUNKS = 8
Z_CHIPS = 12

student_scale = 50.0
teacher_scale = 80.0
loss_scale = 64.0
norm_eps = 1e-06

f32 = jnp.float32
bf16 = jnp.bfloat16
exact = lax.Precision.HIGHEST


def iota(shape, axis):
    return lax.broadcasted_iota(jnp.int32, shape, axis)


def dot(left, right, dims=((1,), (0,)), precision=None):
    return lax.dot_general(left, right, (dims, ((), ())), precision=precision, preferred_element_type=f32)


def segment_mask(rows, count, repeat):
    token = iota((rows, count), 1)
    text = jnp.where(token < QLEN, 0, jnp.where(token < QLEN + PLEN, 1, 2))
    return (text == iota((rows, count), 0) // repeat).astype(f32)


def routing(ids):
    count = ids.shape[1]
    expert = iota((8, count), 0)
    first = expert == ids[0:1, :]
    second = expert == ids[1:2, :]
    hit = jnp.where(first, 1.0, jnp.where(second, 1.0, 0.0))
    before = (iota((count, count), 0) < iota((count, count), 1)).astype(bf16)
    rank = dot(hit.astype(bf16), before)
    return jnp.where(hit > 0.0, rank, -1.0), first, second


def slot_hits(rank, experts, rows):
    count = rank.shape[1]
    slot = iota((rows, count), 0).astype(f32)
    return [(slot == rank[e : e + 1, :]).astype(f32) for e in range(experts)]


def dispatch_kernel(tok_ref, ids_ref, prob_ref, send_ref, *, experts, cap, rows):
    count = tok_ref.shape[0]
    rank, first, second = routing(ids_ref[...])
    probs = prob_ref[...].astype(f32)
    weight = jnp.where(first, probs[0:1, :], jnp.where(second, probs[1:2, :], 0.0))
    wide = slot_hits(rank, experts, 128)
    segs = segment_mask(8, count, 1)
    place = (iota((rows, 8), 0) == cap + iota((rows, 8), 1)).astype(bf16)
    metas = []
    for e in range(experts):
        by_text = (segs * weight[e : e + 1, :]).astype(bf16)
        meta = dot(by_text, wide[e].astype(bf16), ((1,), (1,)))
        metas.append(dot(place, meta.astype(bf16)))
    pick = jnp.concatenate([hits[:rows] for hits in wide], axis=0).astype(bf16)
    width = tok_ref.shape[1]
    send_ref[:, 0:128] = (dot(pick, tok_ref[:, 0:128]) + jnp.concatenate(metas, axis=0)).astype(bf16)
    send_ref[:, 128:width] = dot(pick, tok_ref[:, 128:width]).astype(bf16)


def unit_block(values):
    inverse = lax.rsqrt(jnp.sum(values * values, keepdims=True) + norm_eps)
    return values * inverse, inverse


def to_chunks(row, size):
    which = iota((CHUNKS, size), 0)
    out = jnp.zeros((CHUNKS, size), f32)
    for j in range(CHUNKS):
        out = jnp.where(which == j, row[:, j * size : (j + 1) * size], out)
    return out


def combine_kernel(
    ret_ref, ids_ref, prob_ref, tq_ref, tp_ref, pos_ref, moe_ref, unit_ref, inv_ref, qs_ref, ps_ref, *, experts, rows
):
    count = ids_ref.shape[1]
    width = ret_ref.shape[1]
    size = width // CHUNKS
    rank, first, second = routing(ids_ref[...])
    probs = prob_ref[...].astype(f32)
    weight = jnp.where(first, probs[0:1, :], jnp.where(second, probs[1:2, :], 0.0))
    hits = slot_hits(rank, experts, rows)
    mix = jnp.concatenate([hits[e] * weight[e : e + 1, :] for e in range(experts)], axis=0).astype(bf16)
    moe = dot(mix, ret_ref[...], ((0,), (0,))).astype(bf16)
    moe_ref[...] = moe
    member = segment_mask(SEGS * CHUNKS, count, CHUNKS).astype(bf16)
    chunk = iota((SEGS * CHUNKS, size), 0) % CHUNKS
    pooled = jnp.zeros((SEGS * CHUNKS, size), f32)
    for j in range(CHUNKS):
        pooled = jnp.where(chunk == j, dot(member, moe[:, j * size : (j + 1) * size]), pooled)
    query, query_inv = unit_block(pooled[0:8] * (1.0 / QLEN))
    pass_a, pass_a_inv = unit_block(pooled[8:16] * (1.0 / PLEN))
    pass_b, pass_b_inv = unit_block(pooled[16:24] * (1.0 / PLEN))
    unit_ref[...] = jnp.concatenate([query, pass_a, pass_b], axis=0)
    inv_ref[...] = jnp.concatenate(
        [jnp.broadcast_to(inverse, (8, 128)) for inverse in (query_inv, pass_a_inv, pass_b_inv)], axis=0
    )
    teach_q = unit_block(to_chunks(tq_ref[...].astype(f32), size))[0]
    teach_p = tp_ref[...].astype(f32)
    teach_a = unit_block(to_chunks(teach_p[0:1], size))[0]
    teach_b = unit_block(to_chunks(teach_p[1:2], size))[0]
    pos = pos_ref[0, 0]
    lane = iota((8, size), 1)
    marks = jnp.where(lane == 0, (pos >> 4).astype(f32), jnp.where(lane == 1, (pos & 15).astype(f32), 0.0))
    queries = jnp.concatenate([query, teach_q, marks], axis=0).astype(bf16)
    passages = jnp.concatenate([pass_a, pass_b, teach_a, teach_b], axis=0).astype(bf16)
    for peer in range(qs_ref.shape[0]):
        qs_ref[peer] = queries
    for peer in range(ps_ref.shape[0]):
        ps_ref[peer] = passages


def passage_of(col):
    return (col // 32) * 2 + (col % 16) // 8


def score_kernel(q_ref, p_ref, me_ref, sent_ref, saved_ref, *, peers):
    q_rows = q_ref.shape[0]
    p_rows, size = p_ref.shape
    valid_count = p_rows // 16
    queries = q_ref[...]
    passages = p_ref[...]
    products = dot(queries, passages, ((1,), (1,)))
    row = iota((q_rows, p_rows), 0)
    col = iota((q_rows, p_rows), 1)
    wanted = jnp.where(col % 32 < 16, 0, 1)
    products = jnp.where((row % 24 // 8 == wanted) & (row % 8 == col % 8), products, 0.0)
    products = jnp.sum(products.reshape(3 * peers, 8, p_rows), axis=1)
    join = (passage_of(iota((p_rows, 128), 0)) == iota((p_rows, 128), 1)).astype(f32)
    scores = dot(products, join, precision=exact)
    pick_row = iota((2 * peers, 3 * peers), 0)
    pick = (iota((2 * peers, 3 * peers), 1) == 3 * (pick_row % peers) + pick_row // peers).astype(f32)
    scores = dot(pick, scores, precision=exact)
    student = student_scale * scores[0:peers]
    teacher = teacher_scale * scores[peers : 2 * peers]
    mark_pick = (iota((peers, q_rows), 1) == 24 * iota((peers, q_rows), 0) + 16).astype(bf16)
    marks = dot(mark_pick, queries)
    pos = (16.0 * marks[:, 0:1] + marks[:, 1:2]).astype(jnp.int32)
    lane = iota((peers, 128), 1)
    number = (lane // 2) * (2 * peers) + lane % 2 + 2 * me_ref[0, 0]
    valid = lane < valid_count
    is_pos = jnp.where(valid & (number == pos), 1.0, 0.0)
    student_exp = jnp.where(valid, jnp.exp(student), 0.0)
    teacher_exp = jnp.where(valid, jnp.exp(teacher), 0.0)
    saved_ref[0] = student_exp
    saved_ref[1] = teacher_exp
    saved_ref[2] = is_pos
    parts = (student_exp, teacher_exp, teacher_exp * (teacher - student), is_pos * student)
    sums = jnp.zeros((peers, 128), f32)
    for n, part in enumerate(parts):
        rest = jnp.sum(part, axis=1, keepdims=True)
        for piece in range(3):
            head = rest.astype(bf16).astype(f32)
            sums = jnp.where(lane == 4 * piece + n, head, sums)
            rest = rest - head
    sums = jnp.concatenate([sums[0 : peers // 2], sums[peers // 2 : peers]], axis=1)
    if sums.shape[0] < 8:
        sums = jnp.concatenate([sums] + [jnp.zeros_like(sums)] * (8 // sums.shape[0] - 1), axis=0)
    sums = sums.astype(bf16)
    weights = jnp.concatenate([student_exp, teacher_exp, is_pos], axis=0).astype(bf16)
    row = iota((q_rows, 3 * peers), 0)
    spread = (iota((q_rows, 3 * peers), 1) == (row % 24 // 8) * peers + row // 24).astype(bf16)
    join = (iota((128, p_rows), 0) == passage_of(iota((128, p_rows), 1))).astype(bf16)
    mixing = dot(dot(spread, weights).astype(bf16), join)
    row = iota((q_rows, p_rows), 0)
    mixing = jnp.where((col % 32 < 16) & (row % 8 == col % 8), mixing, 0.0).astype(bf16)
    mixed = dot(mixing, passages)
    for peer in range(peers):
        sent_ref[peer, 0:24, :] = mixed[24 * peer : 24 * peer + 24].astype(bf16)
        sent_ref[peer, 24:32, :] = sums


def coeff_kernel(got_ref, saved_ref, q_ref, me_ref, dq_ref, dp_ref, loss_ref, *, peers):
    q_rows = q_ref.shape[0]
    rows = dp_ref.shape[0]
    total = got_ref[0].astype(f32)
    for peer in range(1, peers):
        total = total + got_ref[peer].astype(f32)
    half = peers // 2

    def quantity(n):
        cols = []
        for side in (0, 128):
            at = side + n
            block = total[24 : 24 + half]
            cols.append(block[:, at : at + 1] + block[:, at + 4 : at + 5] + block[:, at + 8 : at + 9])
        return jnp.concatenate(cols, axis=0)

    student_total, teacher_total, cross, positive = quantity(0), quantity(1), quantity(2), quantity(3)
    loss = 2.0 * jnp.log(student_total) - positive + cross / teacher_total - jnp.log(teacher_total)
    mine = iota((peers, 1), 0) == me_ref[0, 0]
    own = lambda values: jnp.sum(jnp.where(mine, values, 0.0), keepdims=True)
    loss_ref[...] = jnp.broadcast_to(own(loss), (1, 128))
    dq_ref[...] = student_scale * (
        total[0:8] * (2.0 / own(student_total)) - total[8:16] / own(teacher_total) - total[16:24]
    )
    coeffs = (2.0 * saved_ref[0] / student_total - saved_ref[1] / teacher_total - saved_ref[2]).astype(bf16)
    spread = (iota((rows, 128), 0) // CHUNKS == iota((rows, 128), 1)).astype(bf16)
    join = (iota((peers, q_rows), 0) == iota((peers, q_rows), 1) // 24).astype(bf16)
    by_passage = dot(dot(spread, coeffs, ((1,), (1,))).astype(bf16), join)
    row = iota((rows, q_rows), 0)
    col = iota((rows, q_rows), 1)
    by_passage = jnp.where((col % 24 < 8) & (row % 8 == col % 8), by_passage, 0.0).astype(bf16)
    dp_ref[...] = (student_scale * dot(by_passage, q_ref[...])).astype(bf16)


def grad_kernel(dq_ref, dp_ref, unit_ref, inv_ref, grad_ref, sent_ref):
    passage = dp_ref[0].astype(f32)
    for peer in range(1, dp_ref.shape[0]):
        passage = passage + dp_ref[peer].astype(f32)
    parts = []
    for s, (unit_grad, scale) in enumerate(
        ((dq_ref[...], loss_scale / QLEN), (passage[0:8], loss_scale / PLEN), (passage[8:16], loss_scale / PLEN))
    ):
        unit = unit_ref[8 * s : 8 * s + 8, :]
        inverse = inv_ref[8 * s : 8 * s + 8, 0:1]
        along = jnp.sum(unit * unit_grad, keepdims=True)
        parts.append(scale * (inverse * (unit_grad - unit * along)))
    grad = jnp.concatenate(parts, axis=0)
    grad_ref[...] = grad
    for peer in range(sent_ref.shape[0]):
        sent_ref[peer] = grad


def forward_kernel(x_ref, gate_ref, up_ref, down_ref, out_ref, pre_gate_ref, pre_up_ref, acc_ref):
    step = pl.program_id(0)
    rows = x_ref[...]
    pre_gate = dot(rows, gate_ref[...])
    pre_up = dot(rows, up_ref[...])
    pre_gate_ref[...] = pre_gate
    pre_up_ref[...] = pre_up
    hidden = (jax.nn.silu(pre_gate) * pre_up).astype(bf16)
    part = dot(hidden, down_ref[...])

    @pl.when(step == 0)
    def _():
        acc_ref[...] = part

    @pl.when(step > 0)
    def _():
        acc_ref[...] += part

    @pl.when(step == pl.num_programs(0) - 1)
    def _():
        out_ref[...] = acc_ref[...].astype(bf16)


def backward_kernel(
    grad_ref, share_ref, pre_gate_ref, pre_up_ref, gate_ref, up_ref, down_ref, out_ref, acc_ref, *, experts, rows, at
):
    step = pl.program_id(0)
    grad = grad_ref[...]
    texts, size = grad.shape
    block = down_ref.shape[0]
    high = grad.astype(bf16)
    low = (grad - high.astype(f32)).astype(bf16)
    both = jnp.concatenate([high, low], axis=0)
    chunk = iota((2 * texts, block), 0) % CHUNKS
    by_text = jnp.zeros((2 * texts, block), f32)
    for j in range(CHUNKS):
        part = dot(both, down_ref[:, j * size : (j + 1) * size], ((1,), (1,)))
        by_text = jnp.where(chunk == j, part, by_text)
    row = iota((experts * 8, 2 * texts), 0)
    text = iota((experts * 8, 2 * texts), 1) % texts // CHUNKS
    pick = ((text // SEGS == row // 8) & (text % SEGS + at == row % 8)).astype(f32)
    by_text = dot(pick, by_text, precision=exact)
    hidden_grad = jnp.concatenate(
        [
            dot(share_ref[s].astype(f32), by_text[8 * s : 8 * s + 8], ((0,), (0,)), precision=exact)[:rows]
            for s in range(experts)
        ],
        axis=0,
    )
    pre_gate = pre_gate_ref[...]
    sigmoid = jax.nn.sigmoid(pre_gate)
    gate_part = (hidden_grad * pre_up_ref[...] * (sigmoid * (1.0 + pre_gate * (1.0 - sigmoid)))).astype(bf16)
    up_part = (hidden_grad * (pre_gate * sigmoid)).astype(bf16)
    part = dot(gate_part, gate_ref[...], ((1,), (1,))) + dot(up_part, up_ref[...], ((1,), (1,)))

    @pl.when(step == 0)
    def _():
        acc_ref[...] = part

    @pl.when(step > 0)
    def _():
        acc_ref[...] += part

    @pl.when(step == pl.num_programs(0) - 1)
    def _():
        out_ref[...] = acc_ref[...].astype(bf16)


def gate_grad_kernel(ret_ref, ids_ref, grad_ref, out_ref, *, experts, rows):
    count = ids_ref.shape[1]
    size = ret_ref.shape[1] // CHUNKS
    slots = ret_ref.shape[0]
    rank, first, second = routing(ids_ref[...])
    grad = grad_ref[...]
    high = grad.astype(bf16)
    low = (grad - high.astype(f32)).astype(bf16)
    both = jnp.concatenate([high.astype(f32), low.astype(f32)], axis=0).astype(bf16)
    n = 2 * SEGS * CHUNKS
    chunk = iota((n, slots), 0) % CHUNKS
    acc = jnp.zeros((n, slots), f32)
    for j in range(CHUNKS):
        part = dot(both, ret_ref[:, j * size : (j + 1) * size], ((1,), (1,)))
        acc = jnp.where(chunk == j, part, acc)
    gather = (iota((8, n), 1) // CHUNKS % SEGS == iota((8, n), 0)).astype(f32)
    by_slot = dot(gather, acc, precision=exact)
    hits = slot_hits(rank, experts, rows)
    texts = segment_mask(8, count, 1)
    results = []
    for named in (first, second):
        named = jnp.where(named, 1.0, 0.0)
        pick = jnp.concatenate([hits[e] * named[e : e + 1, :] for e in range(experts)], axis=0)
        results.append(jnp.sum(texts * dot(by_slot, pick, precision=exact), axis=0, keepdims=True))
    out_ref[...] = jnp.where(iota((2, count), 0) == 0, results[0], results[1])


def token_grad_kernel(back_ref, ids_ref, out_ref, *, experts, rows):
    rank, _, _ = routing(ids_ref[...])
    pick = jnp.concatenate(slot_hits(rank, experts, rows), axis=0).astype(bf16)
    out_ref[...] = dot(pick, back_ref[...], ((0,), (0,))).astype(bf16)


def vmem(count):
    return [pl.BlockSpec(memory_space=pltpu.VMEM)] * count


SMEM = pl.BlockSpec(memory_space=pltpu.SMEM)


def shape_of(*dims, dtype=f32):
    return jax.ShapeDtypeStruct(dims, dtype)


def exchange(values, axis):
    return lax.all_to_all(values, axis, split_axis=0, concat_axis=0, tiled=True)


def shards(
    tokens,
    expert_ids,
    gate_probs,
    w_gate,
    w_up,
    w_down,
    teacher_queries,
    teacher_passages,
    positives,
):
    experts = lax.axis_size("expert")
    peers = lax.axis_size("yc")
    chips = lax.axis_size("z")
    count, width = tokens.shape
    size = width // CHUNKS
    top = expert_ids.shape[1]
    cap = min(count, (count * top * 33 + 32 * experts - 1) // (32 * experts))
    rows = (cap + SEGS + 7) // 8 * 8
    slots = experts * rows
    ids = expert_ids.T
    probs = gate_probs.T
    me = lax.axis_index("yc").astype(jnp.int32).reshape(1, 1)
    gate_mat = w_gate[0]
    up_mat = w_up[0]
    down_mat = w_down[0]

    sent = pl.pallas_call(
        functools.partial(dispatch_kernel, experts=experts, cap=cap, rows=rows),
        out_shape=shape_of(slots, width, dtype=bf16),
        in_specs=vmem(3),
        out_specs=vmem(1)[0],
        name="dispatch",
    )(tokens, ids, probs)
    arrived = exchange(sent.reshape(experts, rows, width), "expert")
    hidden_size = gate_mat.shape[1]
    block = 256
    whole = lambda *dims: pl.BlockSpec(dims, lambda i: (0,) * len(dims))
    wide = pl.BlockSpec((width, block), lambda i: (0, i))
    tall = pl.BlockSpec((block, width), lambda i: (i, 0))
    pre = pl.BlockSpec((slots, block), lambda i: (0, i))
    expert_out, pre_gate, pre_up = pl.pallas_call(
        forward_kernel,
        grid=(hidden_size // block,),
        out_shape=(
            shape_of(slots, width, dtype=bf16),
            shape_of(slots, hidden_size),
            shape_of(slots, hidden_size),
        ),
        in_specs=[whole(slots, width), wide, wide, tall],
        out_specs=(whole(slots, width), pre, pre),
        scratch_shapes=[pltpu.VMEM((slots, width), f32)],
        name="expert_forward",
    )(arrived.reshape(slots, width), gate_mat, up_mat, down_mat)
    returned = exchange(expert_out.reshape(experts, rows, width), "expert").reshape(slots, width)

    moe_out, unit, inverse, q_sent, p_sent = pl.pallas_call(
        functools.partial(combine_kernel, experts=experts, rows=rows),
        out_shape=(
            shape_of(count, width, dtype=bf16),
            shape_of(SEGS * CHUNKS, size),
            shape_of(SEGS * CHUNKS, 128),
            shape_of(peers, 24, size, dtype=bf16),
            shape_of(chips, 32, size, dtype=bf16),
        ),
        in_specs=vmem(5) + [SMEM],
        out_specs=tuple(vmem(5)),
        name="combine",
    )(returned, ids, probs, teacher_queries[0], teacher_passages[0], positives)
    q_all = exchange(q_sent, "yc").reshape(peers * 24, size)
    p_all = exchange(p_sent, "z").reshape(chips * 32, size)
    mixed_sent, saved = pl.pallas_call(
        functools.partial(score_kernel, peers=peers),
        out_shape=(shape_of(peers, 32, size, dtype=bf16), shape_of(3, peers, 128)),
        in_specs=vmem(2) + [SMEM],
        out_specs=tuple(vmem(2)),
        name="score",
    )(q_all, p_all, me)
    mixed = exchange(mixed_sent, "yc")
    dq, dp_sent, loss = pl.pallas_call(
        functools.partial(coeff_kernel, peers=peers),
        out_shape=(shape_of(CHUNKS, size), shape_of(chips * 16, size, dtype=bf16), shape_of(1, 128)),
        in_specs=vmem(3) + [SMEM],
        out_specs=tuple(vmem(3)),
        name="coeff",
    )(mixed, saved, q_all, me)
    dp = exchange(dp_sent.reshape(chips, 2 * CHUNKS, size), "z")
    grad, grad_sent = pl.pallas_call(
        grad_kernel,
        out_shape=(shape_of(SEGS * CHUNKS, size), shape_of(experts, SEGS * CHUNKS, size)),
        in_specs=vmem(4),
        out_specs=tuple(vmem(2)),
        name="text_grad",
    )(dq, dp, unit, inverse)
    grad_all = exchange(grad_sent, "expert").reshape(experts * SEGS * CHUNKS, size)
    row_grad = pl.pallas_call(
        functools.partial(backward_kernel, experts=experts, rows=rows, at=cap % 8),
        grid=(hidden_size // block,),
        out_shape=shape_of(slots, width, dtype=bf16),
        in_specs=[
            whole(experts * SEGS * CHUNKS, size),
            pl.BlockSpec((experts, 8, 128), lambda i: (0, cap // 8, 0)),
            pre,
            pre,
            wide,
            wide,
            tall,
        ],
        out_specs=whole(slots, width),
        scratch_shapes=[pltpu.VMEM((slots, width), f32)],
        name="expert_backward",
    )(grad_all, arrived, pre_gate, pre_up, gate_mat, up_mat, down_mat)
    back = exchange(row_grad.reshape(experts, rows, width), "expert").reshape(slots, width)
    gate_grad = pl.pallas_call(
        functools.partial(gate_grad_kernel, experts=experts, rows=rows),
        out_shape=shape_of(top, count),
        in_specs=vmem(3),
        out_specs=vmem(1)[0],
        name="gate_grad",
    )(returned, ids, grad)
    token_grad = pl.pallas_call(
        functools.partial(token_grad_kernel, experts=experts, rows=rows),
        out_shape=shape_of(count, width, dtype=bf16),
        in_specs=vmem(2),
        out_specs=vmem(1)[0],
        name="token_grad",
    )(back, ids)
    return (moe_out, token_grad, gate_grad.T, loss[:, :1])


def solution(mesh):
    dp, expert = mesh.devices.shape
    chips = Z_CHIPS if dp % Z_CHIPS == 0 else 2
    grid = Mesh(np.asarray(mesh.devices).reshape(chips, dp // chips, expert), ("z", "yc", "expert"))
    every = ("z", "yc", "expert")
    in_specs = (
        P(every, None),
        P(every, None),
        P(every, None),
        P("expert", None, None),
        P("expert", None, None),
        P("expert", None, None),
        P("expert", ("z", "yc"), None),
        P("expert", ("z", "yc"), None),
        P("expert", ("z", "yc")),
    )
    out_specs = (
        P(every, None),
        P(every, None),
        P(every, None),
        P("expert", ("z", "yc")),
    )
    return jax.shard_map(shards, mesh=grid, in_specs=in_specs, out_specs=out_specs, check_vma=False)
```

```python
import functools

import jax
import jax.numpy as jnp
import numpy as np
from jax import lax
from jax.experimental import pallas as pl
from jax.experimental.pallas import tpu as pltpu
from jax.sharding import Mesh
from jax.sharding import PartitionSpec as P

QLEN = 32
PLEN = 48
SEGS = 3
CHUNKS = 8
Z_CHIPS = 12

student_scale = 50.0
teacher_scale = 80.0
loss_scale = 64.0
norm_eps = 1e-06

f32 = jnp.float32
bf16 = jnp.bfloat16
exact = lax.Precision.HIGHEST


def iota(shape, axis):
    return lax.broadcasted_iota(jnp.int32, shape, axis)


def dot(left, right, dims=((1,), (0,)), precision=None):
    return lax.dot_general(left, right, (dims, ((), ())), precision=precision, preferred_element_type=f32)


def segment_mask(rows, count, repeat):
    token = iota((rows, count), 1)
    text = jnp.where(token < QLEN, 0, jnp.where(token < QLEN + PLEN, 1, 2))
    return (text == iota((rows, count), 0) // repeat).astype(f32)


def routing(ids):
    count = ids.shape[1]
    expert = iota((8, count), 0)
    first = expert == ids[0:1, :]
    second = expert == ids[1:2, :]
    hit = jnp.where(first, 1.0, jnp.where(second, 1.0, 0.0))
    before = (iota((count, count), 0) < iota((count, count), 1)).astype(bf16)
    rank = dot(hit.astype(bf16), before)
    return jnp.where(hit > 0.0, rank, -1.0), first, second


def slot_hits(rank, experts, rows):
    count = rank.shape[1]
    slot = iota((rows, count), 0).astype(f32)
    return [(slot == rank[e : e + 1, :]).astype(f32) for e in range(experts)]


def dispatch_kernel(tok_ref, ids_ref, prob_ref, send_ref, *, experts, cap, rows):
    count = tok_ref.shape[0]
    rank, first, second = routing(ids_ref[...])
    probs = prob_ref[...].astype(f32)
    weight = jnp.where(first, probs[0:1, :], jnp.where(second, probs[1:2, :], 0.0))
    wide = slot_hits(rank, experts, 128)
    segs = segment_mask(8, count, 1)
    place = (iota((rows, 8), 0) == cap + iota((rows, 8), 1)).astype(bf16)
    metas = []
    for e in range(experts):
        by_text = (segs * weight[e : e + 1, :]).astype(bf16)
        meta = dot(by_text, wide[e].astype(bf16), ((1,), (1,)))
        metas.append(dot(place, meta.astype(bf16)))
    pick = jnp.concatenate([hits[:rows] for hits in wide], axis=0).astype(bf16)
    width = tok_ref.shape[1]
    send_ref[:, 0:128] = (dot(pick, tok_ref[:, 0:128]) + jnp.concatenate(metas, axis=0)).astype(bf16)
    send_ref[:, 128:width] = dot(pick, tok_ref[:, 128:width]).astype(bf16)


def unit_block(values):
    inverse = lax.rsqrt(jnp.sum(values * values, keepdims=True) + norm_eps)
    return values * inverse, inverse


def to_chunks(row, size):
    which = iota((CHUNKS, size), 0)
    out = jnp.zeros((CHUNKS, size), f32)
    for j in range(CHUNKS):
        out = jnp.where(which == j, row[:, j * size : (j + 1) * size], out)
    return out


def combine_kernel(ret_ref, ids_ref, prob_ref, moe_ref, *, experts, rows):
    rank, first, second = routing(ids_ref[...])
    probs = prob_ref[...].astype(f32)
    weight = jnp.where(first, probs[0:1, :], jnp.where(second, probs[1:2, :], 0.0))
    hits = slot_hits(rank, experts, rows)
    mix = jnp.concatenate([hits[e] * weight[e : e + 1, :] for e in range(experts)], axis=0).astype(bf16)
    moe_ref[...] = dot(mix, ret_ref[...], ((0,), (0,))).astype(bf16)


def text_kernel(pool_ref, tq_ref, tp_ref, pos_ref, unit_ref, inv_ref, qs_ref, ps_ref):
    size = pool_ref.shape[2]
    pooled = pool_ref[0]
    for e in range(1, pool_ref.shape[0]):
        pooled = pooled + pool_ref[e]
    query, query_inv = unit_block(pooled[0:8] * (1.0 / QLEN))
    pass_a, pass_a_inv = unit_block(pooled[8:16] * (1.0 / PLEN))
    pass_b, pass_b_inv = unit_block(pooled[16:24] * (1.0 / PLEN))
    unit_ref[...] = jnp.concatenate([query, pass_a, pass_b], axis=0)
    inv_ref[...] = jnp.concatenate(
        [jnp.broadcast_to(inverse, (8, 128)) for inverse in (query_inv, pass_a_inv, pass_b_inv)], axis=0
    )
    teach_q = unit_block(to_chunks(tq_ref[...].astype(f32), size))[0]
    teach_p = tp_ref[...].astype(f32)
    teach_a = unit_block(to_chunks(teach_p[0:1], size))[0]
    teach_b = unit_block(to_chunks(teach_p[1:2], size))[0]
    pos = pos_ref[0, 0]
    lane = iota((8, size), 1)
    marks = jnp.where(lane == 0, (pos >> 4).astype(f32), jnp.where(lane == 1, (pos & 15).astype(f32), 0.0))
    queries = jnp.concatenate([query, teach_q, marks], axis=0).astype(bf16)
    passages = jnp.concatenate([pass_a, pass_b, teach_a, teach_b], axis=0).astype(bf16)
    for peer in range(qs_ref.shape[0]):
        qs_ref[peer] = queries
    for peer in range(ps_ref.shape[0]):
        ps_ref[peer] = passages


def passage_of(col):
    return (col // 32) * 2 + (col % 16) // 8


def score_kernel(q_ref, p_ref, me_ref, sent_ref, saved_ref, *, peers):
    q_rows = q_ref.shape[0]
    p_rows, size = p_ref.shape
    valid_count = p_rows // 16
    queries = q_ref[...]
    passages = p_ref[...]
    products = dot(queries, passages, ((1,), (1,)))
    row = iota((q_rows, p_rows), 0)
    col = iota((q_rows, p_rows), 1)
    wanted = jnp.where(col % 32 < 16, 0, 1)
    products = jnp.where((row % 24 // 8 == wanted) & (row % 8 == col % 8), products, 0.0)
    products = jnp.sum(products.reshape(3 * peers, 8, p_rows), axis=1)
    join = (passage_of(iota((p_rows, 128), 0)) == iota((p_rows, 128), 1)).astype(f32)
    scores = dot(products, join, precision=exact)
    pick_row = iota((2 * peers, 3 * peers), 0)
    pick = (iota((2 * peers, 3 * peers), 1) == 3 * (pick_row % peers) + pick_row // peers).astype(f32)
    scores = dot(pick, scores, precision=exact)
    student = student_scale * scores[0:peers]
    teacher = teacher_scale * scores[peers : 2 * peers]
    mark_pick = (iota((peers, q_rows), 1) == 24 * iota((peers, q_rows), 0) + 16).astype(bf16)
    marks = dot(mark_pick, queries)
    pos = (16.0 * marks[:, 0:1] + marks[:, 1:2]).astype(jnp.int32)
    lane = iota((peers, 128), 1)
    number = (lane // 2) * (2 * peers) + lane % 2 + 2 * me_ref[0, 0]
    valid = lane < valid_count
    is_pos = jnp.where(valid & (number == pos), 1.0, 0.0)
    student_exp = jnp.where(valid, jnp.exp(student), 0.0)
    teacher_exp = jnp.where(valid, jnp.exp(teacher), 0.0)
    saved_ref[0] = student_exp
    saved_ref[1] = teacher_exp
    saved_ref[2] = is_pos
    parts = (student_exp, teacher_exp, teacher_exp * (teacher - student), is_pos * student)
    sums = jnp.zeros((peers, 128), f32)
    for n, part in enumerate(parts):
        rest = jnp.sum(part, axis=1, keepdims=True)
        for piece in range(3):
            head = rest.astype(bf16).astype(f32)
            sums = jnp.where(lane == 4 * piece + n, head, sums)
            rest = rest - head
    sums = jnp.concatenate([sums[0 : peers // 2], sums[peers // 2 : peers]], axis=1)
    if sums.shape[0] < 8:
        sums = jnp.concatenate([sums] + [jnp.zeros_like(sums)] * (8 // sums.shape[0] - 1), axis=0)
    sums = sums.astype(bf16)
    weights = jnp.concatenate([student_exp, teacher_exp, is_pos], axis=0).astype(bf16)
    row = iota((q_rows, 3 * peers), 0)
    spread = (iota((q_rows, 3 * peers), 1) == (row % 24 // 8) * peers + row // 24).astype(bf16)
    join = (iota((128, p_rows), 0) == passage_of(iota((128, p_rows), 1))).astype(bf16)
    mixing = dot(dot(spread, weights).astype(bf16), join)
    row = iota((q_rows, p_rows), 0)
    mixing = jnp.where((col % 32 < 16) & (row % 8 == col % 8), mixing, 0.0).astype(bf16)
    mixed = dot(mixing, passages)
    for peer in range(peers):
        sent_ref[peer, 0:24, :] = mixed[24 * peer : 24 * peer + 24].astype(bf16)
        sent_ref[peer, 24:32, :] = sums


def coeff_kernel(got_ref, saved_ref, q_ref, me_ref, dq_ref, dp_ref, loss_ref, *, peers):
    q_rows = q_ref.shape[0]
    rows = dp_ref.shape[0]
    total = got_ref[0].astype(f32)
    for peer in range(1, peers):
        total = total + got_ref[peer].astype(f32)
    half = peers // 2

    def quantity(n):
        cols = []
        for side in (0, 128):
            at = side + n
            block = total[24 : 24 + half]
            cols.append(block[:, at : at + 1] + block[:, at + 4 : at + 5] + block[:, at + 8 : at + 9])
        return jnp.concatenate(cols, axis=0)

    student_total, teacher_total, cross, positive = quantity(0), quantity(1), quantity(2), quantity(3)
    loss = 2.0 * jnp.log(student_total) - positive + cross / teacher_total - jnp.log(teacher_total)
    mine = iota((peers, 1), 0) == me_ref[0, 0]
    own = lambda values: jnp.sum(jnp.where(mine, values, 0.0), keepdims=True)
    loss_ref[...] = jnp.broadcast_to(own(loss), (1, 128))
    dq_ref[...] = student_scale * (
        total[0:8] * (2.0 / own(student_total)) - total[8:16] / own(teacher_total) - total[16:24]
    )
    coeffs = (2.0 * saved_ref[0] / student_total - saved_ref[1] / teacher_total - saved_ref[2]).astype(bf16)
    spread = (iota((rows, 128), 0) // CHUNKS == iota((rows, 128), 1)).astype(bf16)
    join = (iota((peers, q_rows), 0) == iota((peers, q_rows), 1) // 24).astype(bf16)
    by_passage = dot(dot(spread, coeffs, ((1,), (1,))).astype(bf16), join)
    row = iota((rows, q_rows), 0)
    col = iota((rows, q_rows), 1)
    by_passage = jnp.where((col % 24 < 8) & (row % 8 == col % 8), by_passage, 0.0).astype(bf16)
    dp_ref[...] = (student_scale * dot(by_passage, q_ref[...])).astype(bf16)


def grad_kernel(dq_ref, dp_ref, unit_ref, inv_ref, grad_ref, sent_ref):
    passage = dp_ref[0].astype(f32)
    for peer in range(1, dp_ref.shape[0]):
        passage = passage + dp_ref[peer].astype(f32)
    parts = []
    for s, (unit_grad, scale) in enumerate(
        ((dq_ref[...], loss_scale / QLEN), (passage[0:8], loss_scale / PLEN), (passage[8:16], loss_scale / PLEN))
    ):
        unit = unit_ref[8 * s : 8 * s + 8, :]
        inverse = inv_ref[8 * s : 8 * s + 8, 0:1]
        along = jnp.sum(unit * unit_grad, keepdims=True)
        parts.append(scale * (inverse * (unit_grad - unit * along)))
    grad = jnp.concatenate(parts, axis=0)
    grad_ref[...] = grad
    for peer in range(sent_ref.shape[0]):
        sent_ref[peer] = grad


def fetch(sources, targets, sems):
    copies = [pltpu.make_async_copy(a, b, sems.at[n]) for n, (a, b) in enumerate(zip(sources, targets))]
    for copy in copies:
        copy.start()
    return copies


def forward_kernel(
    x_ref,
    gate_ref,
    up_hbm,
    down_hbm,
    out_ref,
    pool_ref,
    gate_slope_ref,
    up_slope_ref,
    share_ref,
    up_ref,
    down_ref,
    sems,
    *,
    experts,
    at,
):
    half = down_ref.shape[0] // 2
    width = down_ref.shape[1]
    size = width // CHUNKS
    copies = fetch(
        (up_hbm, down_hbm.at[0:half], down_hbm.at[half:]), (up_ref, down_ref.at[0:half], down_ref.at[half:]), sems
    )
    slots = x_ref.shape[0]
    rows = slots // experts
    row = iota((8, 128), 0)
    lane = iota((8, 128), 1)
    wanted = (row >= at) & (row < at + SEGS) & (lane < rows)
    shares = []
    for s in range(experts):
        share = jnp.where(wanted, x_ref[rows * (s + 1) - 8 : rows * (s + 1), 0:128].astype(f32), 0.0)
        share_ref[s] = share
        shares.append(share[:, 0:rows].astype(bf16))
    pre_gate = dot(x_ref[...], gate_ref[...])
    sigmoid = jax.nn.sigmoid(pre_gate)
    active = pre_gate * sigmoid
    slope = sigmoid * (1.0 + pre_gate * (1.0 - sigmoid))
    up_slope_ref[...] = active.astype(bf16)
    copies[0].wait()
    pre_up = dot(x_ref[...], up_ref[...])
    gate_slope_ref[...] = (pre_up * slope).astype(bf16)
    hidden = active * pre_up
    text = jnp.concatenate(
        [dot(shares[s], hidden[rows * s : rows * (s + 1)].astype(bf16)) for s in range(experts)], axis=0
    )
    high = text.astype(bf16).astype(f32)
    stacked = jnp.concatenate([hidden, high, text - high], axis=0).astype(bf16)
    copies[1].wait()
    part = dot(stacked[:, 0:half], down_ref[0:half])
    copies[2].wait()
    part = part + dot(stacked[:, half:], down_ref[half:])
    out_ref[...] = part[0:slots].astype(bf16)
    text = part[slots : slots + 8 * experts] + part[slots + 8 * experts :]
    for s in range(experts):
        for t in range(SEGS):
            one = 8 * s + at + t
            pool_ref[s, 8 * t : 8 * t + 8, :] = to_chunks(text[one : one + 1], size)


def backward_kernel(
    grad_ref, share_ref, gate_slope_ref, up_slope_ref, gate_ref, up_hbm, down_hbm, out_ref, up_ref, down_ref, sems, *, experts, rows, at
):
    copies = fetch((down_hbm, up_hbm), (down_ref, up_ref), sems)
    grad = grad_ref[...]
    texts, size = grad.shape
    block = down_ref.shape[0]
    high = grad.astype(bf16)
    low = (grad - high.astype(f32)).astype(bf16)
    both = jnp.concatenate([high, low], axis=0)
    chunk = iota((2 * texts, block), 0) % CHUNKS
    by_text = jnp.zeros((2 * texts, block), f32)
    copies[0].wait()
    for j in range(CHUNKS):
        part = dot(both, down_ref[:, j * size : (j + 1) * size], ((1,), (1,)))
        by_text = jnp.where(chunk == j, part, by_text)
    row = iota((experts * 8, 2 * texts), 0)
    text = iota((experts * 8, 2 * texts), 1) % texts // CHUNKS
    pick = ((text // SEGS == row // 8) & (text % SEGS + at == row % 8)).astype(f32)
    by_text = dot(pick, by_text, precision=exact)
    hidden_grad = jnp.concatenate(
        [
            dot(share_ref[s], by_text[8 * s : 8 * s + 8], ((0,), (0,)), precision=exact)[:rows]
            for s in range(experts)
        ],
        axis=0,
    )
    gate_part = (hidden_grad * gate_slope_ref[...].astype(f32)).astype(bf16)
    up_part = (hidden_grad * up_slope_ref[...].astype(f32)).astype(bf16)
    part = dot(gate_part, gate_ref[...], ((1,), (1,)))
    copies[1].wait()
    out_ref[...] = (part + dot(up_part, up_ref[...], ((1,), (1,)))).astype(bf16)


def gate_grad_kernel(ret_ref, ids_ref, grad_ref, out_ref, *, experts, rows):
    count = ids_ref.shape[1]
    size = ret_ref.shape[1] // CHUNKS
    slots = ret_ref.shape[0]
    rank, first, second = routing(ids_ref[...])
    grad = grad_ref[...]
    high = grad.astype(bf16)
    low = (grad - high.astype(f32)).astype(bf16)
    both = jnp.concatenate([high.astype(f32), low.astype(f32)], axis=0).astype(bf16)
    n = 2 * SEGS * CHUNKS
    chunk = iota((n, slots), 0) % CHUNKS
    acc = jnp.zeros((n, slots), f32)
    for j in range(CHUNKS):
        part = dot(both, ret_ref[:, j * size : (j + 1) * size], ((1,), (1,)))
        acc = jnp.where(chunk == j, part, acc)
    gather = (iota((8, n), 1) // CHUNKS % SEGS == iota((8, n), 0)).astype(f32)
    by_slot = dot(gather, acc, precision=exact)
    hits = slot_hits(rank, experts, rows)
    texts = segment_mask(8, count, 1)
    results = []
    for named in (first, second):
        named = jnp.where(named, 1.0, 0.0)
        pick = jnp.concatenate([hits[e] * named[e : e + 1, :] for e in range(experts)], axis=0)
        results.append(jnp.sum(texts * dot(by_slot, pick, precision=exact), axis=0, keepdims=True))
    out_ref[...] = jnp.where(iota((2, count), 0) == 0, results[0], results[1])


def token_grad_kernel(back_ref, ids_ref, out_ref, *, experts, rows):
    rank, _, _ = routing(ids_ref[...])
    pick = jnp.concatenate(slot_hits(rank, experts, rows), axis=0).astype(bf16)
    out_ref[...] = dot(pick, back_ref[...], ((0,), (0,))).astype(bf16)


LIMIT = pltpu.CompilerParams(vmem_limit_bytes=52 * 1024 * 1024)


def near(values):
    return pltpu.with_memory_space_constraint(values, pltpu.VMEM)


def vmem(count):
    return [pl.BlockSpec(memory_space=pltpu.VMEM)] * count


HBM = pl.BlockSpec(memory_space=pltpu.HBM)
SMEM = pl.BlockSpec(memory_space=pltpu.SMEM)


def shape_of(*dims, dtype=f32):
    return jax.ShapeDtypeStruct(dims, dtype)


def hand_back(values, experts, rows):
    me = lax.axis_index("expert")
    blocks = values.reshape(experts, rows, values.shape[1])
    take = lambda n: lax.dynamic_index_in_dim(blocks, n, 0, keepdims=False)
    got = take(me)[None]
    out = lax.dynamic_update_slice(jnp.zeros_like(blocks), got, (me, 0, 0))
    for step in range(1, experts):
        pairs = [(n, (n + step) % experts) for n in range(experts)]
        got = lax.ppermute(take((me + step) % experts), "expert", pairs)
        out = lax.dynamic_update_slice(out, got[None], ((me - step) % experts, 0, 0))
    return out.reshape(values.shape)


def exchange(values, axis):
    return lax.all_to_all(values, axis, split_axis=0, concat_axis=0, tiled=True)


def shards(
    tokens,
    expert_ids,
    gate_probs,
    w_gate,
    w_up,
    w_down,
    teacher_queries,
    teacher_passages,
    positives,
):
    experts = lax.axis_size("expert")
    peers = lax.axis_size("yc")
    chips = lax.axis_size("z")
    count, width = tokens.shape
    size = width // CHUNKS
    top = expert_ids.shape[1]
    cap = min(count, (count * top * 33 + 32 * experts - 1) // (32 * experts))
    rows = (cap + SEGS + 7) // 8 * 8
    slots = experts * rows
    ids = expert_ids.T
    probs = gate_probs.T
    me = lax.axis_index("yc").astype(jnp.int32).reshape(1, 1)
    gate_mat = w_gate[0]
    up_mat = w_up[0]
    down_mat = w_down[0]

    sent = pl.pallas_call(
        functools.partial(dispatch_kernel, experts=experts, cap=cap, rows=rows),
        out_shape=shape_of(slots, width, dtype=bf16),
        in_specs=vmem(3),
        out_specs=vmem(1)[0],
        name="dispatch",
    )(tokens, ids, probs)
    arrived = exchange(sent.reshape(experts, rows, width), "expert")
    hidden_size = gate_mat.shape[1]
    buffers = [pltpu.VMEM((width, hidden_size), bf16), pltpu.VMEM((hidden_size, width), bf16)]
    expert_out, pool_sent, gate_slope, up_slope, share = pl.pallas_call(
        functools.partial(forward_kernel, experts=experts, at=cap - (rows - 8)),
        out_shape=(
            shape_of(slots, width, dtype=bf16),
            shape_of(experts, SEGS * CHUNKS, size),
            shape_of(slots, hidden_size, dtype=bf16),
            shape_of(slots, hidden_size, dtype=bf16),
            shape_of(experts, 8, 128),
        ),
        in_specs=vmem(2) + [HBM] * 2,
        out_specs=tuple(vmem(5)),
        scratch_shapes=buffers + [pltpu.SemaphoreType.DMA((3,))],
        name="expert_forward",
        compiler_params=LIMIT,
    )(arrived.reshape(slots, width), near(gate_mat), up_mat, down_mat)
    pool = exchange(pool_sent, "expert")
    unit, inverse, q_sent, p_sent = pl.pallas_call(
        text_kernel,
        out_shape=(
            shape_of(SEGS * CHUNKS, size),
            shape_of(SEGS * CHUNKS, 128),
            shape_of(peers, 24, size, dtype=bf16),
            shape_of(chips, 32, size, dtype=bf16),
        ),
        in_specs=vmem(3) + [SMEM],
        out_specs=tuple(vmem(4)),
        name="text",
    )(pool, teacher_queries[0], teacher_passages[0], positives)
    with jax.named_scope("q_gather"):
        q_all = exchange(q_sent, "yc").reshape(peers * 24, size)
    with jax.named_scope("p_gather"):
        p_all = exchange(p_sent, "z").reshape(chips * 32, size)
    with jax.named_scope("expert_back"):
        returned = hand_back(expert_out, experts, rows)
    moe_out = pl.pallas_call(
        functools.partial(combine_kernel, experts=experts, rows=rows),
        out_shape=shape_of(count, width, dtype=bf16),
        in_specs=vmem(3),
        out_specs=vmem(1)[0],
        name="combine",
    )(returned, ids, probs)
    mixed_sent, saved = pl.pallas_call(
        functools.partial(score_kernel, peers=peers),
        out_shape=(shape_of(peers, 32, size, dtype=bf16), shape_of(3, peers, 128)),
        in_specs=vmem(2) + [SMEM],
        out_specs=tuple(vmem(2)),
        name="score",
    )(q_all, p_all, me)
    mixed = exchange(mixed_sent, "yc")
    dq, dp_sent, loss = pl.pallas_call(
        functools.partial(coeff_kernel, peers=peers),
        out_shape=(shape_of(CHUNKS, size), shape_of(chips * 16, size, dtype=bf16), shape_of(1, 128)),
        in_specs=vmem(3) + [SMEM],
        out_specs=tuple(vmem(3)),
        name="coeff",
    )(mixed, saved, q_all, me)
    dp = exchange(dp_sent.reshape(chips, 2 * CHUNKS, size), "z")
    grad, grad_sent = pl.pallas_call(
        grad_kernel,
        out_shape=(shape_of(SEGS * CHUNKS, size), shape_of(experts, SEGS * CHUNKS, size)),
        in_specs=vmem(4),
        out_specs=tuple(vmem(2)),
        name="text_grad",
    )(dq, dp, unit, inverse)
    grad_all = exchange(grad_sent, "expert").reshape(experts * SEGS * CHUNKS, size)
    row_grad = pl.pallas_call(
        functools.partial(backward_kernel, experts=experts, rows=rows, at=cap - (rows - 8)),
        out_shape=shape_of(slots, width, dtype=bf16),
        in_specs=vmem(5) + [HBM] * 2,
        out_specs=vmem(1)[0],
        scratch_shapes=buffers + [pltpu.SemaphoreType.DMA((2,))],
        name="expert_backward",
        compiler_params=LIMIT,
    )(grad_all, share, gate_slope, up_slope, near(gate_mat), up_mat, down_mat)
    back = exchange(row_grad.reshape(experts, rows, width), "expert").reshape(slots, width)
    gate_grad = pl.pallas_call(
        functools.partial(gate_grad_kernel, experts=experts, rows=rows),
        out_shape=shape_of(top, count),
        in_specs=vmem(3),
        out_specs=vmem(1)[0],
        name="gate_grad",
    )(returned, ids, grad)
    token_grad = pl.pallas_call(
        functools.partial(token_grad_kernel, experts=experts, rows=rows),
        out_shape=shape_of(count, width, dtype=bf16),
        in_specs=vmem(2),
        out_specs=vmem(1)[0],
        name="token_grad",
    )(near(back), ids)
    return (moe_out, token_grad, gate_grad.T, loss[:, :1])


def solution(mesh):
    dp, expert = mesh.devices.shape
    chips = Z_CHIPS if dp % Z_CHIPS == 0 else 2
    grid = Mesh(np.asarray(mesh.devices).reshape(chips, dp // chips, expert), ("z", "yc", "expert"))
    every = ("z", "yc", "expert")
    in_specs = (
        P(every, None),
        P(every, None),
        P(every, None),
        P("expert", None, None),
        P("expert", None, None),
        P("expert", None, None),
        P("expert", ("z", "yc"), None),
        P("expert", ("z", "yc"), None),
        P("expert", ("z", "yc")),
    )
    out_specs = (
        P(every, None),
        P(every, None),
        P(every, None),
        P("expert", ("z", "yc")),
    )
    return jax.shard_map(shards, mesh=grid, in_specs=in_specs, out_specs=out_specs, check_vma=False)
```

```python
import functools

import jax
import jax.numpy as jnp
import numpy as np
from jax import lax
from jax.experimental import pallas as pl
from jax.experimental.pallas import tpu as pltpu
from jax.sharding import Mesh
from jax.sharding import PartitionSpec as P

QLEN = 32
PLEN = 48
SEGS = 3
CHUNKS = 8
Z_CHIPS = 12

student_scale = 50.0
teacher_scale = 80.0
loss_scale = 64.0
norm_eps = 1e-06

f32 = jnp.float32
bf16 = jnp.bfloat16
exact = lax.Precision.HIGHEST


def iota(shape, axis):
    return lax.broadcasted_iota(jnp.int32, shape, axis)


def dot(left, right, dims=((1,), (0,)), precision=None):
    return lax.dot_general(left, right, (dims, ((), ())), precision=precision, preferred_element_type=f32)


def segment_mask(rows, count, repeat):
    token = iota((rows, count), 1)
    text = jnp.where(token < QLEN, 0, jnp.where(token < QLEN + PLEN, 1, 2))
    return (text == iota((rows, count), 0) // repeat).astype(f32)


def routing(ids):
    count = ids.shape[1]
    expert = iota((8, count), 0)
    first = expert == ids[0:1, :]
    second = expert == ids[1:2, :]
    hit = jnp.where(first, 1.0, jnp.where(second, 1.0, 0.0))
    before = (iota((count, count), 0) < iota((count, count), 1)).astype(bf16)
    rank = dot(hit.astype(bf16), before)
    return jnp.where(hit > 0.0, rank, -1.0), first, second


def slot_hits(rank, experts, rows):
    count = rank.shape[1]
    slot = iota((rows, count), 0).astype(f32)
    return [(slot == rank[e : e + 1, :]).astype(f32) for e in range(experts)]


def dispatch_kernel(tok_ref, ids_ref, prob_ref, send_ref, *, experts, cap, rows):
    count = tok_ref.shape[0]
    rank, first, second = routing(ids_ref[...])
    probs = prob_ref[...].astype(f32)
    weight = jnp.where(first, probs[0:1, :], jnp.where(second, probs[1:2, :], 0.0))
    wide = slot_hits(rank, experts, 128)
    segs = segment_mask(8, count, 1)
    place = (iota((rows, 8), 0) == cap + iota((rows, 8), 1)).astype(bf16)
    metas = []
    for e in range(experts):
        by_text = (segs * weight[e : e + 1, :]).astype(bf16)
        meta = dot(by_text, wide[e].astype(bf16), ((1,), (1,)))
        metas.append(dot(place, meta.astype(bf16)))
    pick = jnp.concatenate([hits[:rows] for hits in wide], axis=0).astype(bf16)
    width = tok_ref.shape[1]
    send_ref[:, 0:128] = (dot(pick, tok_ref[:, 0:128]) + jnp.concatenate(metas, axis=0)).astype(bf16)
    send_ref[:, 128:width] = dot(pick, tok_ref[:, 128:width]).astype(bf16)


def unit_block(values):
    inverse = lax.rsqrt(jnp.sum(values * values, keepdims=True) + norm_eps)
    return values * inverse, inverse


def to_chunks(row, size):
    which = iota((CHUNKS, size), 0)
    out = jnp.zeros((CHUNKS, size), f32)
    for j in range(CHUNKS):
        out = jnp.where(which == j, row[:, j * size : (j + 1) * size], out)
    return out


def combine_kernel(ret_ref, ids_ref, prob_ref, moe_ref, *, experts, rows):
    rank, first, second = routing(ids_ref[...])
    probs = prob_ref[...].astype(f32)
    weight = jnp.where(first, probs[0:1, :], jnp.where(second, probs[1:2, :], 0.0))
    hits = slot_hits(rank, experts, rows)
    mix = jnp.concatenate([hits[e] * weight[e : e + 1, :] for e in range(experts)], axis=0).astype(bf16)
    moe_ref[...] = dot(mix, ret_ref[...], ((0,), (0,))).astype(bf16)


def text_kernel(pool_ref, tq_ref, tp_ref, pos_ref, unit_ref, inv_ref, qs_ref, ps_ref):
    size = pool_ref.shape[2]
    pooled = pool_ref[0]
    for e in range(1, pool_ref.shape[0]):
        pooled = pooled + pool_ref[e]
    query, query_inv = unit_block(pooled[0:8] * (1.0 / QLEN))
    pass_a, pass_a_inv = unit_block(pooled[8:16] * (1.0 / PLEN))
    pass_b, pass_b_inv = unit_block(pooled[16:24] * (1.0 / PLEN))
    unit_ref[...] = jnp.concatenate([query, pass_a, pass_b], axis=0)
    inv_ref[...] = jnp.concatenate(
        [jnp.broadcast_to(inverse, (8, 128)) for inverse in (query_inv, pass_a_inv, pass_b_inv)], axis=0
    )
    teach_q = unit_block(to_chunks(tq_ref[...].astype(f32), size))[0]
    teach_p = tp_ref[...].astype(f32)
    teach_a = unit_block(to_chunks(teach_p[0:1], size))[0]
    teach_b = unit_block(to_chunks(teach_p[1:2], size))[0]
    pos = pos_ref[0, 0]
    lane = iota((8, size), 1)
    marks = jnp.where(lane == 0, (pos >> 4).astype(f32), jnp.where(lane == 1, (pos & 15).astype(f32), 0.0))
    queries = jnp.concatenate([query, teach_q, marks], axis=0).astype(bf16)
    passages = jnp.concatenate([pass_a, pass_b, teach_a, teach_b], axis=0).astype(bf16)
    for peer in range(qs_ref.shape[0]):
        qs_ref[peer] = queries
    for peer in range(ps_ref.shape[0]):
        ps_ref[peer] = passages


def passage_of(col):
    return (col // 32) * 2 + (col % 16) // 8


def score_kernel(q_ref, p_ref, me_ref, sent_ref, saved_ref, *, peers):
    q_rows = q_ref.shape[0]
    p_rows, size = p_ref.shape
    valid_count = p_rows // 16
    queries = q_ref[...]
    passages = p_ref[...]
    products = dot(queries, passages, ((1,), (1,)))
    row = iota((q_rows, p_rows), 0)
    col = iota((q_rows, p_rows), 1)
    wanted = jnp.where(col % 32 < 16, 0, 1)
    products = jnp.where((row % 24 // 8 == wanted) & (row % 8 == col % 8), products, 0.0)
    products = jnp.sum(products.reshape(3 * peers, 8, p_rows), axis=1)
    join = (passage_of(iota((p_rows, 128), 0)) == iota((p_rows, 128), 1)).astype(f32)
    scores = dot(products, join, precision=exact)
    pick_row = iota((2 * peers, 3 * peers), 0)
    pick = (iota((2 * peers, 3 * peers), 1) == 3 * (pick_row % peers) + pick_row // peers).astype(f32)
    scores = dot(pick, scores, precision=exact)
    student = student_scale * scores[0:peers]
    teacher = teacher_scale * scores[peers : 2 * peers]
    mark_pick = (iota((peers, q_rows), 1) == 24 * iota((peers, q_rows), 0) + 16).astype(bf16)
    marks = dot(mark_pick, queries)
    pos = (16.0 * marks[:, 0:1] + marks[:, 1:2]).astype(jnp.int32)
    lane = iota((peers, 128), 1)
    number = (lane // 2) * (2 * peers) + lane % 2 + 2 * me_ref[0, 0]
    valid = lane < valid_count
    is_pos = jnp.where(valid & (number == pos), 1.0, 0.0)
    student_exp = jnp.where(valid, jnp.exp(student), 0.0)
    teacher_exp = jnp.where(valid, jnp.exp(teacher), 0.0)
    saved_ref[0] = student_exp
    saved_ref[1] = teacher_exp
    saved_ref[2] = is_pos
    parts = (student_exp, teacher_exp, teacher_exp * (teacher - student), is_pos * student)
    sums = jnp.zeros((peers, 128), f32)
    for n, part in enumerate(parts):
        rest = jnp.sum(part, axis=1, keepdims=True)
        for piece in range(3):
            head = rest.astype(bf16).astype(f32)
            sums = jnp.where(lane == 4 * piece + n, head, sums)
            rest = rest - head
    sums = jnp.concatenate([sums[0 : peers // 2], sums[peers // 2 : peers]], axis=1)
    if sums.shape[0] < 8:
        sums = jnp.concatenate([sums] + [jnp.zeros_like(sums)] * (8 // sums.shape[0] - 1), axis=0)
    sums = sums.astype(bf16)
    weights = jnp.concatenate([student_exp, teacher_exp, is_pos], axis=0).astype(bf16)
    row = iota((q_rows, 3 * peers), 0)
    spread = (iota((q_rows, 3 * peers), 1) == (row % 24 // 8) * peers + row // 24).astype(bf16)
    join = (iota((128, p_rows), 0) == passage_of(iota((128, p_rows), 1))).astype(bf16)
    mixing = dot(dot(spread, weights).astype(bf16), join)
    row = iota((q_rows, p_rows), 0)
    mixing = jnp.where((col % 32 < 16) & (row % 8 == col % 8), mixing, 0.0).astype(bf16)
    mixed = dot(mixing, passages)
    for peer in range(peers):
        sent_ref[peer, 0:24, :] = mixed[24 * peer : 24 * peer + 24].astype(bf16)
        sent_ref[peer, 24:32, :] = sums


def coeff_kernel(got_ref, saved_ref, q_ref, me_ref, dq_ref, dp_ref, loss_ref, *, peers):
    q_rows = q_ref.shape[0]
    rows = dp_ref.shape[0]
    total = got_ref[0].astype(f32)
    for peer in range(1, peers):
        total = total + got_ref[peer].astype(f32)
    half = peers // 2

    def quantity(n):
        cols = []
        for side in (0, 128):
            at = side + n
            block = total[24 : 24 + half]
            cols.append(block[:, at : at + 1] + block[:, at + 4 : at + 5] + block[:, at + 8 : at + 9])
        return jnp.concatenate(cols, axis=0)

    student_total, teacher_total, cross, positive = quantity(0), quantity(1), quantity(2), quantity(3)
    loss = 2.0 * jnp.log(student_total) - positive + cross / teacher_total - jnp.log(teacher_total)
    mine = iota((peers, 1), 0) == me_ref[0, 0]
    own = lambda values: jnp.sum(jnp.where(mine, values, 0.0), keepdims=True)
    loss_ref[...] = jnp.broadcast_to(own(loss), (1, 128))
    dq_ref[...] = student_scale * (
        total[0:8] * (2.0 / own(student_total)) - total[8:16] / own(teacher_total) - total[16:24]
    )
    coeffs = (2.0 * saved_ref[0] / student_total - saved_ref[1] / teacher_total - saved_ref[2]).astype(bf16)
    spread = (iota((rows, 128), 0) // CHUNKS == iota((rows, 128), 1)).astype(bf16)
    join = (iota((peers, q_rows), 0) == iota((peers, q_rows), 1) // 24).astype(bf16)
    by_passage = dot(dot(spread, coeffs, ((1,), (1,))).astype(bf16), join)
    row = iota((rows, q_rows), 0)
    col = iota((rows, q_rows), 1)
    by_passage = jnp.where((col % 24 < 8) & (row % 8 == col % 8), by_passage, 0.0).astype(bf16)
    dp_ref[...] = (student_scale * dot(by_passage, q_ref[...])).astype(bf16)


def grad_kernel(dq_ref, dp_ref, unit_ref, inv_ref, grad_ref, sent_ref):
    passage = dp_ref[0].astype(f32)
    for peer in range(1, dp_ref.shape[0]):
        passage = passage + dp_ref[peer].astype(f32)
    parts = []
    for s, (unit_grad, scale) in enumerate(
        ((dq_ref[...], loss_scale / QLEN), (passage[0:8], loss_scale / PLEN), (passage[8:16], loss_scale / PLEN))
    ):
        unit = unit_ref[8 * s : 8 * s + 8, :]
        inverse = inv_ref[8 * s : 8 * s + 8, 0:1]
        along = jnp.sum(unit * unit_grad, keepdims=True)
        parts.append(scale * (inverse * (unit_grad - unit * along)))
    grad = jnp.concatenate(parts, axis=0)
    grad_ref[...] = grad
    high = grad.astype(bf16).astype(f32)
    split = jnp.concatenate([high, grad - high], axis=0).astype(bf16)
    texts, size = grad.shape
    row = iota((8, 2 * texts), 0)
    first = row // SEGS * texts + row % SEGS * CHUNKS
    for j in range(CHUNKS):
        pick = ((iota((8, 2 * texts), 1) == first + j) & (row < 2 * SEGS)).astype(bf16)
        rows = dot(pick, split).astype(bf16)
        for peer in range(sent_ref.shape[0]):
            sent_ref[peer, :, size * j : size * (j + 1)] = rows


def fetch(sources, targets, sems, base):
    copies = [pltpu.make_async_copy(a, b, sems.at[base + n]) for n, (a, b) in enumerate(zip(sources, targets))]
    for copy in copies:
        copy.start()
    return copies


def forward_kernel(
    x_ref,
    gate_ref,
    up_hbm,
    down_hbm,
    out_hbm,
    pool_ref,
    gate_slope_hbm,
    up_slope_hbm,
    share_ref,
    up_ref,
    down_ref,
    out_ref,
    gate_slope_ref,
    up_slope_ref,
    sems,
    *,
    experts,
    at,
):
    width = down_ref.shape[1]
    half = width // 2
    size = width // CHUNKS
    top = (up_hbm.at[0:half], up_ref.at[0:half])
    low = (up_hbm.at[half:], up_ref.at[half:])
    copies = fetch((top[0], low[0], down_hbm), (top[1], low[1], down_ref), sems, 0)
    slots = x_ref.shape[0]
    rows = slots // experts
    row = iota((8, 128), 0)
    lane = iota((8, 128), 1)
    wanted = (row >= at) & (row < at + SEGS) & (lane < rows)
    pick_row = iota((8, 8), 0)
    pick = ((iota((8, 8), 1) == at + pick_row % SEGS) & (pick_row < 2 * SEGS)).astype(bf16)
    shares = []
    for s in range(experts):
        share = jnp.where(wanted, x_ref[rows * (s + 1) - 8 : rows * (s + 1), 0:128].astype(f32), 0.0)
        share = dot(pick, share.astype(bf16))
        share_ref[s] = share
        shares.append(share[:, 0:rows].astype(bf16))
    pre_gate = dot(x_ref[...], gate_ref[...])
    sigmoid = jax.nn.sigmoid(pre_gate)
    active = pre_gate * sigmoid
    slope = sigmoid * (1.0 + pre_gate * (1.0 - sigmoid))
    up_slope_ref[...] = active.astype(bf16)
    copies[0].wait()
    pre_up = dot(x_ref[:, 0:half], up_ref[0:half])
    copies[1].wait()
    pre_up = pre_up + dot(x_ref[:, half:], up_ref[half:])
    gate_slope_ref[...] = (pre_up * slope).astype(bf16)
    sent = fetch((up_slope_ref, gate_slope_ref), (up_slope_hbm, gate_slope_hbm), sems, 3)
    hidden = active * pre_up
    text = jnp.concatenate(
        [dot(shares[s], hidden[rows * s : rows * (s + 1)].astype(bf16)) for s in range(experts)], axis=0
    )
    high = text.astype(bf16).astype(f32)
    stacked = jnp.concatenate([hidden, high, text - high], axis=0).astype(bf16)
    copies[2].wait()
    texts = []
    for n in range(2):
        part = dot(stacked, down_ref[:, half * n : half * (n + 1)])
        out_ref[:, half * n : half * (n + 1)] = part[0:slots].astype(bf16)
        target = out_hbm.at[:, half * n : half * (n + 1)]
        sent += fetch((out_ref.at[:, half * n : half * (n + 1)],), (target,), sems, 5 + n)
        texts.append(part[slots : slots + 8 * experts] + part[slots + 8 * experts :])
    text = jnp.concatenate(texts, axis=1)
    for s in range(experts):
        for t in range(SEGS):
            one = 8 * s + t
            pool_ref[s, 8 * t : 8 * t + 8, :] = to_chunks(text[one : one + 1], size)
    for copy in sent:
        copy.wait()


def backward_kernel(
    grad_ref,
    share_ref,
    gate_slope_ref,
    up_slope_ref,
    down_ref,
    gate_hbm,
    up_hbm,
    out_hbm,
    gate_ref,
    up_ref,
    out_ref,
    sems,
    *,
    experts,
    rows,
):
    width = gate_ref.shape[0]
    half = width // 2
    parts = [(hbm.at[half * n : half * (n + 1)], ref.at[half * n : half * (n + 1)])
             for n in range(2) for hbm, ref in ((gate_hbm, gate_ref), (up_hbm, up_ref))]
    copies = fetch([part[0] for part in parts], [part[1] for part in parts], sems, 0)
    by_text = dot(grad_ref[...], down_ref[...], ((1,), (1,)))
    high = by_text.astype(bf16).astype(f32)
    low = by_text - high
    blocks = []
    for s in range(experts):
        share = jnp.concatenate([share_ref[s], share_ref[s]], axis=0).astype(bf16)
        split = jnp.concatenate([high[8 * s : 8 * s + 8], low[8 * s : 8 * s + 8]], axis=0).astype(bf16)
        blocks.append(dot(share, split, ((0,), (0,)))[:rows])
    hidden_grad = jnp.concatenate(blocks, axis=0)
    gate_part = (hidden_grad * gate_slope_ref[...].astype(f32)).astype(bf16)
    up_part = (hidden_grad * up_slope_ref[...].astype(f32)).astype(bf16)
    sent = []
    for n in range(2):
        span = slice(half * n, half * (n + 1))
        copies[2 * n].wait()
        part = dot(gate_part, gate_ref[span], ((1,), (1,)))
        copies[2 * n + 1].wait()
        out_ref[:, span] = (part + dot(up_part, up_ref[span], ((1,), (1,)))).astype(bf16)
        sent += fetch((out_ref.at[:, span],), (out_hbm.at[:, span],), sems, 4 + n)
    for copy in sent:
        copy.wait()


def gate_grad_kernel(ret_ref, ids_ref, grad_ref, out_ref, *, experts, rows):
    count = ids_ref.shape[1]
    size = ret_ref.shape[1] // CHUNKS
    slots = ret_ref.shape[0]
    rank, first, second = routing(ids_ref[...])
    grad = grad_ref[...]
    high = grad.astype(bf16)
    low = (grad - high.astype(f32)).astype(bf16)
    both = jnp.concatenate([high.astype(f32), low.astype(f32)], axis=0).astype(bf16)
    n = 2 * SEGS * CHUNKS
    chunk = iota((n, slots), 0) % CHUNKS
    acc = jnp.zeros((n, slots), f32)
    for j in range(CHUNKS):
        part = dot(both, ret_ref[:, j * size : (j + 1) * size], ((1,), (1,)))
        acc = jnp.where(chunk == j, part, acc)
    gather = (iota((8, n), 1) // CHUNKS % SEGS == iota((8, n), 0)).astype(f32)
    by_slot = dot(gather, acc, precision=exact)
    hits = slot_hits(rank, experts, rows)
    texts = segment_mask(8, count, 1)
    results = []
    for named in (first, second):
        named = jnp.where(named, 1.0, 0.0)
        pick = jnp.concatenate([hits[e] * named[e : e + 1, :] for e in range(experts)], axis=0)
        results.append(jnp.sum(texts * dot(by_slot, pick, precision=exact), axis=0, keepdims=True))
    out_ref[...] = jnp.where(iota((2, count), 0) == 0, results[0], results[1])


def token_grad_kernel(back_ref, ids_ref, out_ref, *, experts, rows):
    rank, _, _ = routing(ids_ref[...])
    pick = jnp.concatenate(slot_hits(rank, experts, rows), axis=0).astype(bf16)
    out_ref[...] = dot(pick, back_ref[...], ((0,), (0,))).astype(bf16)


LIMIT = pltpu.CompilerParams(vmem_limit_bytes=52 * 1024 * 1024)


def near(values):
    return pltpu.with_memory_space_constraint(values, pltpu.VMEM)


def vmem(count):
    return [pl.BlockSpec(memory_space=pltpu.VMEM)] * count


HBM = pl.BlockSpec(memory_space=pltpu.HBM)
SMEM = pl.BlockSpec(memory_space=pltpu.SMEM)


def shape_of(*dims, dtype=f32):
    return jax.ShapeDtypeStruct(dims, dtype)


def hand_back(values, experts, rows):
    me = lax.axis_index("expert")
    blocks = values.reshape(experts, rows, values.shape[1])
    take = lambda n: lax.dynamic_index_in_dim(blocks, n, 0, keepdims=False)
    got = take(me)[None]
    out = lax.dynamic_update_slice(jnp.zeros_like(blocks), got, (me, 0, 0))
    for step in range(1, experts):
        pairs = [(n, (n + step) % experts) for n in range(experts)]
        got = lax.ppermute(take((me + step) % experts), "expert", pairs)
        out = lax.dynamic_update_slice(out, got[None], ((me - step) % experts, 0, 0))
    return out.reshape(values.shape)


def exchange(values, axis):
    return lax.all_to_all(values, axis, split_axis=0, concat_axis=0, tiled=True)


def shards(
    tokens,
    expert_ids,
    gate_probs,
    w_gate,
    w_up,
    w_down,
    teacher_queries,
    teacher_passages,
    positives,
):
    experts = lax.axis_size("expert")
    peers = lax.axis_size("yc")
    chips = lax.axis_size("z")
    count, width = tokens.shape
    size = width // CHUNKS
    top = expert_ids.shape[1]
    cap = min(count, (count * top * 33 + 32 * experts - 1) // (32 * experts))
    rows = (cap + SEGS + 7) // 8 * 8
    slots = experts * rows
    ids = expert_ids.T
    probs = gate_probs.T
    me = lax.axis_index("yc").astype(jnp.int32).reshape(1, 1)
    gate_mat = w_gate[0]
    up_mat = w_up[0]
    down_mat = w_down[0]

    sent = pl.pallas_call(
        functools.partial(dispatch_kernel, experts=experts, cap=cap, rows=rows),
        out_shape=shape_of(slots, width, dtype=bf16),
        in_specs=vmem(3),
        out_specs=vmem(1)[0],
        name="dispatch",
    )(tokens, ids, probs)
    arrived = exchange(sent.reshape(experts, rows, width), "expert")
    hidden_size = gate_mat.shape[1]
    wide = pltpu.VMEM((width, hidden_size), bf16)
    tall = pltpu.VMEM((hidden_size, width), bf16)
    slope = pltpu.VMEM((slots, hidden_size), bf16)
    outgoing = pltpu.VMEM((slots, width), bf16)
    expert_out, pool_sent, gate_slope, up_slope, share = pl.pallas_call(
        functools.partial(forward_kernel, experts=experts, at=cap - (rows - 8)),
        out_shape=(
            shape_of(slots, width, dtype=bf16),
            shape_of(experts, SEGS * CHUNKS, size),
            shape_of(slots, hidden_size, dtype=bf16),
            shape_of(slots, hidden_size, dtype=bf16),
            shape_of(experts, 8, 128),
        ),
        in_specs=vmem(2) + [HBM] * 2,
        out_specs=(HBM, vmem(1)[0], HBM, HBM, vmem(1)[0]),
        scratch_shapes=[wide, tall, outgoing, slope, slope, pltpu.SemaphoreType.DMA((7,))],
        name="expert_forward",
        compiler_params=LIMIT,
    )(arrived.reshape(slots, width), near(gate_mat), up_mat, down_mat)
    pool = exchange(pool_sent, "expert")
    unit, inverse, q_sent, p_sent = pl.pallas_call(
        text_kernel,
        out_shape=(
            shape_of(SEGS * CHUNKS, size),
            shape_of(SEGS * CHUNKS, 128),
            shape_of(peers, 24, size, dtype=bf16),
            shape_of(chips, 32, size, dtype=bf16),
        ),
        in_specs=vmem(3) + [SMEM],
        out_specs=tuple(vmem(4)),
        name="text",
    )(near(pool), teacher_queries[0], teacher_passages[0], positives)
    with jax.named_scope("q_gather"):
        q_all = exchange(q_sent, "yc").reshape(peers * 24, size)
    with jax.named_scope("p_gather"):
        p_all = exchange(p_sent, "z").reshape(chips * 32, size)
    with jax.named_scope("expert_back"):
        returned = hand_back(expert_out, experts, rows)
    moe_out = pl.pallas_call(
        functools.partial(combine_kernel, experts=experts, rows=rows),
        out_shape=shape_of(count, width, dtype=bf16),
        in_specs=vmem(3),
        out_specs=vmem(1)[0],
        name="combine",
    )(returned, ids, probs)
    mixed_sent, saved = pl.pallas_call(
        functools.partial(score_kernel, peers=peers),
        out_shape=(shape_of(peers, 32, size, dtype=bf16), shape_of(3, peers, 128)),
        in_specs=vmem(2) + [SMEM],
        out_specs=tuple(vmem(2)),
        name="score",
    )(q_all, near(p_all), me)
    mixed = exchange(mixed_sent, "yc")
    dq, dp_sent, loss = pl.pallas_call(
        functools.partial(coeff_kernel, peers=peers),
        out_shape=(shape_of(CHUNKS, size), shape_of(chips * 16, size, dtype=bf16), shape_of(1, 128)),
        in_specs=vmem(3) + [SMEM],
        out_specs=tuple(vmem(3)),
        name="coeff",
    )(near(mixed), saved, q_all, me)
    dp = exchange(dp_sent.reshape(chips, 2 * CHUNKS, size), "z")
    grad, grad_sent = pl.pallas_call(
        grad_kernel,
        out_shape=(shape_of(SEGS * CHUNKS, size), shape_of(experts, 8, width, dtype=bf16)),
        in_specs=vmem(4),
        out_specs=tuple(vmem(2)),
        name="text_grad",
    )(dq, near(dp), unit, inverse)
    grad_all = exchange(grad_sent, "expert").reshape(experts * 8, width)
    row_grad = pl.pallas_call(
        functools.partial(backward_kernel, experts=experts, rows=rows),
        out_shape=shape_of(slots, width, dtype=bf16),
        in_specs=vmem(5) + [HBM] * 2,
        out_specs=HBM,
        scratch_shapes=[wide, wide, outgoing, pltpu.SemaphoreType.DMA((6,))],
        name="expert_backward",
        compiler_params=LIMIT,
    )(near(grad_all), share, gate_slope, up_slope, near(down_mat), gate_mat, up_mat)
    back = exchange(row_grad.reshape(experts, rows, width), "expert").reshape(slots, width)
    gate_grad = pl.pallas_call(
        functools.partial(gate_grad_kernel, experts=experts, rows=rows),
        out_shape=shape_of(top, count),
        in_specs=vmem(3),
        out_specs=vmem(1)[0],
        name="gate_grad",
    )(returned, ids, grad)
    token_grad = pl.pallas_call(
        functools.partial(token_grad_kernel, experts=experts, rows=rows),
        out_shape=shape_of(count, width, dtype=bf16),
        in_specs=vmem(2),
        out_specs=vmem(1)[0],
        name="token_grad",
    )(near(back), ids)
    return (moe_out, token_grad, gate_grad.T, loss[:, :1])


def solution(mesh):
    dp, expert = mesh.devices.shape
    chips = Z_CHIPS if dp % Z_CHIPS == 0 else 2
    grid = Mesh(np.asarray(mesh.devices).reshape(chips, dp // chips, expert), ("z", "yc", "expert"))
    every = ("z", "yc", "expert")
    in_specs = (
        P(every, None),
        P(every, None),
        P(every, None),
        P("expert", None, None),
        P("expert", None, None),
        P("expert", None, None),
        P("expert", ("z", "yc"), None),
        P("expert", ("z", "yc"), None),
        P("expert", ("z", "yc")),
    )
    out_specs = (
        P(every, None),
        P(every, None),
        P(every, None),
        P("expert", ("z", "yc")),
    )
    return jax.shard_map(shards, mesh=grid, in_specs=in_specs, out_specs=out_specs, check_vma=False)
```

```python
import functools

import jax
import jax.numpy as jnp
import numpy as np
from jax import lax
from jax.experimental import pallas as pl
from jax.experimental.pallas import tpu as pltpu
from jax.sharding import Mesh
from jax.sharding import PartitionSpec as P

QLEN = 32
PLEN = 48
SEGS = 3
CHUNKS = 8
Z_CHIPS = 12

student_scale = 50.0
teacher_scale = 80.0
loss_scale = 64.0
norm_eps = 1e-06

f32 = jnp.float32
bf16 = jnp.bfloat16
exact = lax.Precision.HIGHEST


def iota(shape, axis):
    return lax.broadcasted_iota(jnp.int32, shape, axis)


def dot(left, right, dims=((1,), (0,)), precision=None):
    return lax.dot_general(left, right, (dims, ((), ())), precision=precision, preferred_element_type=f32)


def segment_mask(rows, count, repeat):
    token = iota((rows, count), 1)
    text = jnp.where(token < QLEN, 0, jnp.where(token < QLEN + PLEN, 1, 2))
    return (text == iota((rows, count), 0) // repeat).astype(f32)


def routing(ids):
    count = ids.shape[1]
    expert = iota((8, count), 0)
    first = expert == ids[0:1, :]
    second = expert == ids[1:2, :]
    hit = jnp.where(first, 1.0, jnp.where(second, 1.0, 0.0))
    before = (iota((count, count), 0) < iota((count, count), 1)).astype(bf16)
    rank = dot(hit.astype(bf16), before)
    return jnp.where(hit > 0.0, rank, -1.0), first, second


def slot_hits(rank, experts, rows):
    count = rank.shape[1]
    slot = iota((rows, count), 0).astype(f32)
    return [(slot == rank[e : e + 1, :]).astype(f32) for e in range(experts)]


def dispatch_kernel(tok_ref, ids_ref, prob_ref, send_hbm, send_ref, sems, *, experts, cap, rows):
    count = tok_ref.shape[0]
    rank, first, second = routing(ids_ref[...])
    probs = prob_ref[...].astype(f32)
    weight = jnp.where(first, probs[0:1, :], jnp.where(second, probs[1:2, :], 0.0))
    wide = slot_hits(rank, experts, 128)
    segs = segment_mask(8, count, 1)
    place = (iota((rows, 8), 0) == cap + iota((rows, 8), 1)).astype(bf16)
    metas = []
    for e in range(experts):
        by_text = (segs * weight[e : e + 1, :]).astype(bf16)
        meta = dot(by_text, wide[e].astype(bf16), ((1,), (1,)))
        metas.append(dot(place, meta.astype(bf16)))
    pick = jnp.concatenate([hits[:rows] for hits in wide], axis=0).astype(bf16)
    width = tok_ref.shape[1]
    step = width // 4
    metas = jnp.concatenate(metas, axis=0)
    sent = []
    for n in range(4):
        span = slice(step * n, step * (n + 1))
        block = dot(pick, tok_ref[:, span])
        if n == 0:
            block = jnp.concatenate([block[:, 0:128] + metas, block[:, 128:]], axis=1)
        send_ref[:, span] = block.astype(bf16)
        sent += fetch((send_ref.at[:, span],), (send_hbm.at[:, span],), sems, n)
    for copy in sent:
        copy.wait()


def unit_block(values):
    inverse = lax.rsqrt(jnp.sum(values * values, keepdims=True) + norm_eps)
    return values * inverse, inverse


def to_chunks(row, size):
    which = iota((CHUNKS, size), 0)
    out = jnp.zeros((CHUNKS, size), f32)
    for j in range(CHUNKS):
        out = jnp.where(which == j, row[:, j * size : (j + 1) * size], out)
    return out


def combine_kernel(ret_ref, ids_ref, prob_ref, moe_ref, *, experts, rows):
    rank, first, second = routing(ids_ref[...])
    probs = prob_ref[...].astype(f32)
    weight = jnp.where(first, probs[0:1, :], jnp.where(second, probs[1:2, :], 0.0))
    hits = slot_hits(rank, experts, rows)
    mix = jnp.concatenate([hits[e] * weight[e : e + 1, :] for e in range(experts)], axis=0).astype(bf16)
    moe_ref[...] = dot(mix, ret_ref[...], ((0,), (0,))).astype(bf16)


def teacher_kernel(_, tq_ref, tp_ref, pos_ref, out_ref):
    size = out_ref.shape[1]
    teach_p = tp_ref[...].astype(f32)
    out_ref[0:8] = unit_block(to_chunks(tq_ref[...].astype(f32), size))[0]
    out_ref[8:16] = unit_block(to_chunks(teach_p[0:1], size))[0]
    out_ref[16:24] = unit_block(to_chunks(teach_p[1:2], size))[0]
    pos = pos_ref[0, 0]
    lane = iota((8, size), 1)
    out_ref[24:32] = jnp.where(lane == 0, (pos >> 4).astype(f32), jnp.where(lane == 1, (pos & 15).astype(f32), 0.0))


def text_kernel(pool_ref, teach_ref, unit_ref, inv_ref, qs_ref, ps_ref):
    pooled = pool_ref[0]
    for e in range(1, pool_ref.shape[0]):
        pooled = pooled + pool_ref[e]
    query, query_inv = unit_block(pooled[0:8] * (1.0 / QLEN))
    pass_a, pass_a_inv = unit_block(pooled[8:16] * (1.0 / PLEN))
    pass_b, pass_b_inv = unit_block(pooled[16:24] * (1.0 / PLEN))
    unit_ref[...] = jnp.concatenate([query, pass_a, pass_b], axis=0)
    inv_ref[...] = jnp.concatenate(
        [jnp.broadcast_to(inverse, (8, 128)) for inverse in (query_inv, pass_a_inv, pass_b_inv)], axis=0
    )
    queries = jnp.concatenate([query, teach_ref[0:8], teach_ref[24:32]], axis=0).astype(bf16)
    passages = jnp.concatenate([pass_a, pass_b, teach_ref[8:24]], axis=0).astype(bf16)
    for peer in range(qs_ref.shape[0]):
        qs_ref[peer] = queries
    for peer in range(ps_ref.shape[0]):
        ps_ref[peer] = passages


def passage_of(col):
    return (col // 32) * 2 + (col % 16) // 8


def score_kernel(_, q_ref, p_ref, me_ref, sent_ref, saved_ref, *, peers):
    q_rows = q_ref.shape[0]
    p_rows, size = p_ref.shape
    valid_count = p_rows // 16
    queries = q_ref[...]
    passages = p_ref[...]
    products = dot(queries, passages, ((1,), (1,)))
    row = iota((q_rows, 1), 0)
    col = iota((1, p_rows), 1)
    place = col % 32
    chunk = place % 8
    key = row % 24
    products = jnp.where(jnp.where(key < 16, key, -1) == jnp.where(place < 16, chunk, 8 + chunk), products, 0.0)
    products = jnp.sum(products.reshape(3 * peers, 8, p_rows), axis=1)
    join = (passage_of(iota((p_rows, 1), 0)) == iota((p_rows, 128), 1)).astype(f32)
    scores = dot(products, join, precision=exact)
    pick_row = iota((2 * peers, 3 * peers), 0)
    pick = (iota((2 * peers, 3 * peers), 1) == 3 * (pick_row % peers) + pick_row // peers).astype(f32)
    scores = dot(pick, scores, precision=exact)
    student = student_scale * scores[0:peers]
    teacher = teacher_scale * scores[peers : 2 * peers]
    mark_pick = (iota((peers, q_rows), 1) == 24 * iota((peers, q_rows), 0) + 16).astype(bf16)
    marks = dot(mark_pick, queries)
    pos = (16.0 * marks[:, 0:1] + marks[:, 1:2]).astype(jnp.int32)
    lane = iota((peers, 128), 1)
    number = (lane // 2) * (2 * peers) + lane % 2 + 2 * me_ref[0, 0]
    valid = lane < valid_count
    is_pos = jnp.where(valid & (number == pos), 1.0, 0.0)
    student_exp = jnp.where(valid, jnp.exp(student), 0.0)
    teacher_exp = jnp.where(valid, jnp.exp(teacher), 0.0)
    saved_ref[0] = student_exp
    saved_ref[1] = teacher_exp
    saved_ref[2] = is_pos
    parts = (student_exp, teacher_exp, teacher_exp * (teacher - student), is_pos * student)
    sums = jnp.zeros((peers, 128), f32)
    for n, part in enumerate(parts):
        rest = jnp.sum(part, axis=1, keepdims=True)
        for piece in range(3):
            head = rest.astype(bf16).astype(f32)
            sums = jnp.where(lane == 4 * piece + n, head, sums)
            rest = rest - head
    sums = jnp.concatenate([sums[0 : peers // 2], sums[peers // 2 : peers]], axis=1)
    if sums.shape[0] < 8:
        sums = jnp.concatenate([sums] + [jnp.zeros_like(sums)] * (8 // sums.shape[0] - 1), axis=0)
    sums = sums.astype(bf16)
    weights = jnp.concatenate([student_exp, teacher_exp, is_pos], axis=0).astype(bf16)
    spread = (iota((q_rows, 3 * peers), 1) == (key // 8) * peers + row // 24).astype(bf16)
    join = (iota((128, p_rows), 0) == passage_of(col)).astype(bf16)
    mixing = dot(dot(spread, weights).astype(bf16), join)
    mixing = jnp.where(row % 8 == jnp.where(place < 16, chunk, -1), mixing, 0.0).astype(bf16)
    mixed = dot(mixing, passages)
    for peer in range(peers):
        sent_ref[peer, 0:24, :] = mixed[24 * peer : 24 * peer + 24].astype(bf16)
        sent_ref[peer, 24:32, :] = sums


def coeff_kernel(got_ref, saved_ref, q_ref, me_ref, dq_ref, dp_ref, loss_ref, *, peers):
    q_rows = q_ref.shape[0]
    rows = dp_ref.shape[0]
    total = got_ref[0].astype(f32)
    for peer in range(1, peers):
        total = total + got_ref[peer].astype(f32)
    half = peers // 2

    def quantity(n):
        cols = []
        for side in (0, 128):
            at = side + n
            block = total[24 : 24 + half]
            cols.append(block[:, at : at + 1] + block[:, at + 4 : at + 5] + block[:, at + 8 : at + 9])
        return jnp.concatenate(cols, axis=0)

    student_total, teacher_total, cross, positive = quantity(0), quantity(1), quantity(2), quantity(3)
    loss = 2.0 * jnp.log(student_total) - positive + cross / teacher_total - jnp.log(teacher_total)
    mine = iota((peers, 1), 0) == me_ref[0, 0]
    own = lambda values: jnp.sum(jnp.where(mine, values, 0.0), keepdims=True)
    loss_ref[...] = jnp.broadcast_to(own(loss), (1, 128))
    dq_ref[...] = student_scale * (
        total[0:8] * (2.0 / own(student_total)) - total[8:16] / own(teacher_total) - total[16:24]
    )
    coeffs = (2.0 * saved_ref[0] / student_total - saved_ref[1] / teacher_total - saved_ref[2]).astype(bf16)
    row = iota((rows, 1), 0)
    col = iota((1, q_rows), 1)
    key = col % 24
    spread = (row // CHUNKS == iota((rows, 128), 1)).astype(bf16)
    join = (iota((peers, q_rows), 0) == col // 24).astype(bf16)
    by_passage = dot(dot(spread, coeffs, ((1,), (1,))).astype(bf16), join)
    by_passage = jnp.where(row % 8 == jnp.where(key < 8, key, -1), by_passage, 0.0).astype(bf16)
    dp_ref[...] = (student_scale * dot(by_passage, q_ref[...])).astype(bf16)


def grad_kernel(dq_ref, dp_ref, unit_ref, inv_ref, grad_ref, sent_ref):
    passage = dp_ref[0].astype(f32)
    for peer in range(1, dp_ref.shape[0]):
        passage = passage + dp_ref[peer].astype(f32)
    parts = []
    for s, (unit_grad, scale) in enumerate(
        ((dq_ref[...], loss_scale / QLEN), (passage[0:8], loss_scale / PLEN), (passage[8:16], loss_scale / PLEN))
    ):
        unit = unit_ref[8 * s : 8 * s + 8, :]
        inverse = inv_ref[8 * s : 8 * s + 8, 0:1]
        along = jnp.sum(unit * unit_grad, keepdims=True)
        parts.append(scale * (inverse * (unit_grad - unit * along)))
    grad = jnp.concatenate(parts, axis=0)
    grad_ref[...] = grad
    high = grad.astype(bf16).astype(f32)
    split = jnp.concatenate([high, grad - high], axis=0).astype(bf16)
    texts, size = grad.shape
    row = iota((8, 2 * texts), 0)
    first = row // SEGS * texts + row % SEGS * CHUNKS
    for j in range(CHUNKS):
        pick = ((iota((8, 2 * texts), 1) == first + j) & (row < 2 * SEGS)).astype(bf16)
        rows = dot(pick, split).astype(bf16)
        for peer in range(sent_ref.shape[0]):
            sent_ref[peer, :, size * j : size * (j + 1)] = rows


def fetch(sources, targets, sems, base):
    copies = [pltpu.make_async_copy(a, b, sems.at[base + n]) for n, (a, b) in enumerate(zip(sources, targets))]
    for copy in copies:
        copy.start()
    return copies


def forward_kernel(
    x_ref,
    gate_ref,
    up_hbm,
    down_hbm,
    hidden_hbm,
    pool_ref,
    gate_slope_hbm,
    up_slope_hbm,
    share_ref,
    up_ref,
    down_ref,
    hidden_ref,
    gate_slope_ref,
    up_slope_ref,
    sems,
    *,
    experts,
    at,
):
    width = down_ref.shape[1]
    size = width // CHUNKS
    half = width // 2
    top = (up_hbm.at[0:half], up_ref.at[0:half])
    low = (up_hbm.at[half:], up_ref.at[half:])
    copies = fetch((top[0], low[0], down_hbm), (top[1], low[1], down_ref), sems, 0)
    slots = x_ref.shape[0]
    rows = slots // experts
    row = iota((8, 128), 0)
    lane = iota((8, 128), 1)
    wanted = (row >= at) & (row < at + SEGS) & (lane < rows)
    pick_row = iota((8, 8), 0)
    pick = ((iota((8, 8), 1) == at + pick_row % SEGS) & (pick_row < 2 * SEGS)).astype(bf16)
    shares = []
    for s in range(experts):
        share = jnp.where(wanted, x_ref[rows * (s + 1) - 8 : rows * (s + 1), 0:128].astype(f32), 0.0)
        share = dot(pick, share.astype(bf16))
        share_ref[s] = share
        shares.append(share[:, 0:rows].astype(bf16))
    pre_gate = dot(x_ref[...], gate_ref[...])
    sigmoid = jax.nn.sigmoid(pre_gate)
    active = pre_gate * sigmoid
    slope = sigmoid * (1.0 + pre_gate * (1.0 - sigmoid))
    up_slope_ref[...] = active.astype(bf16)
    copies[0].wait()
    pre_up = dot(x_ref[:, 0:half], up_ref[0:half])
    copies[1].wait()
    pre_up = pre_up + dot(x_ref[:, half:], up_ref[half:])
    gate_slope_ref[...] = (pre_up * slope).astype(bf16)
    hidden = active * pre_up
    hidden_ref[...] = hidden.astype(bf16)
    sent = fetch(
        (hidden_ref, up_slope_ref, gate_slope_ref), (hidden_hbm, up_slope_hbm, gate_slope_hbm), sems, 3
    )
    text = jnp.concatenate(
        [dot(shares[s], hidden[rows * s : rows * (s + 1)].astype(bf16)) for s in range(experts)], axis=0
    )
    high = text.astype(bf16).astype(f32)
    stacked = jnp.concatenate([high, text - high], axis=0).astype(bf16)
    copies[2].wait()
    part = dot(stacked, down_ref[...])
    text = part[0 : 8 * experts] + part[8 * experts :]
    for s in range(experts):
        for t in range(SEGS):
            one = 8 * s + t
            pool_ref[s, 8 * t : 8 * t + 8, :] = to_chunks(text[one : one + 1], size)
    for copy in sent:
        copy.wait()


def down_kernel(hidden_ref, down_ref, out_ref):
    out_ref[...] = dot(hidden_ref[...], down_ref[...]).astype(bf16)


def backward_kernel(
    grad_ref,
    share_ref,
    gate_slope_ref,
    up_slope_ref,
    down_ref,
    gate_hbm,
    up_hbm,
    out_hbm,
    gate_ref,
    up_ref,
    out_ref,
    sems,
    *,
    experts,
    rows,
):
    width = gate_ref.shape[0]
    half = width // 2
    parts = [(hbm.at[half * n : half * (n + 1)], ref.at[half * n : half * (n + 1)])
             for n in range(2) for hbm, ref in ((gate_hbm, gate_ref), (up_hbm, up_ref))]
    copies = fetch([part[0] for part in parts], [part[1] for part in parts], sems, 0)
    by_text = dot(grad_ref[...], down_ref[...], ((1,), (1,)))
    high = by_text.astype(bf16).astype(f32)
    low = by_text - high
    blocks = []
    for s in range(experts):
        share = jnp.concatenate([share_ref[s], share_ref[s]], axis=0).astype(bf16)
        split = jnp.concatenate([high[8 * s : 8 * s + 8], low[8 * s : 8 * s + 8]], axis=0).astype(bf16)
        blocks.append(dot(share, split, ((0,), (0,)))[:rows])
    hidden_grad = jnp.concatenate(blocks, axis=0)
    gate_part = (hidden_grad * gate_slope_ref[...].astype(f32)).astype(bf16)
    up_part = (hidden_grad * up_slope_ref[...].astype(f32)).astype(bf16)
    sent = []
    for n in range(2):
        span = slice(half * n, half * (n + 1))
        copies[2 * n].wait()
        part = dot(gate_part, gate_ref[span], ((1,), (1,)))
        copies[2 * n + 1].wait()
        out_ref[:, span] = (part + dot(up_part, up_ref[span], ((1,), (1,)))).astype(bf16)
        sent += fetch((out_ref.at[:, span],), (out_hbm.at[:, span],), sems, 4 + n)
    for copy in sent:
        copy.wait()


def gate_grad_kernel(ret_ref, ids_ref, grad_ref, out_ref, *, experts, rows):
    count = ids_ref.shape[1]
    size = ret_ref.shape[1] // CHUNKS
    slots = ret_ref.shape[0]
    rank, first, second = routing(ids_ref[...])
    grad = grad_ref[...]
    high = grad.astype(bf16)
    low = (grad - high.astype(f32)).astype(bf16)
    both = jnp.concatenate([high.astype(f32), low.astype(f32)], axis=0).astype(bf16)
    n = 2 * SEGS * CHUNKS
    chunk = iota((n, slots), 0) % CHUNKS
    acc = jnp.zeros((n, slots), f32)
    for j in range(CHUNKS):
        part = dot(both, ret_ref[:, j * size : (j + 1) * size], ((1,), (1,)))
        acc = jnp.where(chunk == j, part, acc)
    gather = (iota((8, n), 1) // CHUNKS % SEGS == iota((8, n), 0)).astype(f32)
    by_slot = dot(gather, acc, precision=exact)
    hits = slot_hits(rank, experts, rows)
    texts = segment_mask(8, count, 1)
    results = []
    for named in (first, second):
        named = jnp.where(named, 1.0, 0.0)
        pick = jnp.concatenate([hits[e] * named[e : e + 1, :] for e in range(experts)], axis=0)
        results.append(jnp.sum(texts * dot(by_slot, pick, precision=exact), axis=0, keepdims=True))
    out_ref[...] = jnp.where(iota((2, count), 0) == 0, results[0], results[1])


def token_grad_kernel(back_ref, ids_ref, out_ref, *, experts, rows):
    rank, _, _ = routing(ids_ref[...])
    pick = jnp.concatenate(slot_hits(rank, experts, rows), axis=0).astype(bf16)
    out_ref[...] = dot(pick, back_ref[...], ((0,), (0,))).astype(bf16)


LIMIT = pltpu.CompilerParams(vmem_limit_bytes=52 * 1024 * 1024)


def near(values):
    return pltpu.with_memory_space_constraint(values, pltpu.VMEM)


def vmem(count):
    return [pl.BlockSpec(memory_space=pltpu.VMEM)] * count


HBM = pl.BlockSpec(memory_space=pltpu.HBM)
SMEM = pl.BlockSpec(memory_space=pltpu.SMEM)


def shape_of(*dims, dtype=f32):
    return jax.ShapeDtypeStruct(dims, dtype)


def row_blocks(values, experts, rows):
    me = lax.axis_index("expert")
    blocks = values.reshape(experts, rows, values.shape[1])
    take = lambda n: lax.dynamic_index_in_dim(blocks, n % experts, 0, keepdims=False)
    return [take(me + step) for step in range(experts)]


def hand_back(leaving):
    me = lax.axis_index("expert")
    experts = len(leaving)
    out = jnp.zeros((experts,) + leaving[0].shape, leaving[0].dtype)
    for step in range(experts):
        pairs = [(n, (n + step) % experts) for n in range(experts)]
        got = lax.ppermute(leaving[step], "expert", pairs) if step else leaving[0]
        out = lax.dynamic_update_slice(out, got[None], ((me - step) % experts, 0, 0))
    return out.reshape(-1, out.shape[2])


def exchange(values, axis):
    return lax.all_to_all(values, axis, split_axis=0, concat_axis=0, tiled=True)


def shards(
    tokens,
    expert_ids,
    gate_probs,
    w_gate,
    w_up,
    w_down,
    teacher_queries,
    teacher_passages,
    positives,
):
    experts = lax.axis_size("expert")
    peers = lax.axis_size("yc")
    chips = lax.axis_size("z")
    count, width = tokens.shape
    size = width // CHUNKS
    top = expert_ids.shape[1]
    cap = min(count, (count * top * 33 + 32 * experts - 1) // (32 * experts))
    rows = (cap + SEGS + 7) // 8 * 8
    slots = experts * rows
    ids = expert_ids.T
    probs = gate_probs.T
    me = lax.axis_index("yc").astype(jnp.int32).reshape(1, 1)
    gate_mat = w_gate[0]
    up_mat = w_up[0]
    down_mat = w_down[0]

    sent = pl.pallas_call(
        functools.partial(dispatch_kernel, experts=experts, cap=cap, rows=rows),
        out_shape=shape_of(slots, width, dtype=bf16),
        in_specs=vmem(3),
        out_specs=HBM,
        scratch_shapes=[pltpu.VMEM((slots, width), bf16), pltpu.SemaphoreType.DMA((4,))],
        name="dispatch",
    )(tokens, ids, probs)
    teach = pl.pallas_call(
        teacher_kernel,
        out_shape=shape_of(32, size),
        in_specs=[HBM] + vmem(2) + [SMEM],
        out_specs=vmem(1)[0],
        name="teacher",
    )(sent, teacher_queries[0], teacher_passages[0], positives)
    arrived = exchange(sent.reshape(experts, rows, width), "expert")
    hidden_size = gate_mat.shape[1]
    wide = pltpu.VMEM((width, hidden_size), bf16)
    tall = pltpu.VMEM((hidden_size, width), bf16)
    slope = pltpu.VMEM((slots, hidden_size), bf16)
    outgoing = pltpu.VMEM((slots, width), bf16)
    hidden, pool_sent, gate_slope, up_slope, share = pl.pallas_call(
        functools.partial(forward_kernel, experts=experts, at=cap - (rows - 8)),
        out_shape=(
            shape_of(slots, hidden_size, dtype=bf16),
            shape_of(experts, SEGS * CHUNKS, size),
            shape_of(slots, hidden_size, dtype=bf16),
            shape_of(slots, hidden_size, dtype=bf16),
            shape_of(experts, 8, 128),
        ),
        in_specs=vmem(2) + [HBM] * 2,
        out_specs=(HBM, vmem(1)[0], HBM, HBM, vmem(1)[0]),
        scratch_shapes=[wide, tall, slope, slope, slope, pltpu.SemaphoreType.DMA((6,))],
        name="expert_forward",
        compiler_params=LIMIT,
    )(arrived.reshape(slots, width), near(gate_mat), up_mat, down_mat)
    expert_out = pl.pallas_call(
        down_kernel,
        out_shape=shape_of(slots, width, dtype=bf16),
        in_specs=vmem(2),
        out_specs=vmem(1)[0],
        name="expert_down",
    )(hidden, down_mat)
    pool = exchange(pool_sent, "expert")
    unit, inverse, q_sent, p_sent = pl.pallas_call(
        text_kernel,
        out_shape=(
            shape_of(SEGS * CHUNKS, size),
            shape_of(SEGS * CHUNKS, 128),
            shape_of(peers, 24, size, dtype=bf16),
            shape_of(chips, 32, size, dtype=bf16),
        ),
        in_specs=vmem(2),
        out_specs=tuple(vmem(4)),
        name="text",
    )(near(pool), teach)
    with jax.named_scope("q_gather"):
        q_all = exchange(q_sent, "yc").reshape(peers * 24, size)
    with jax.named_scope("p_gather"):
        p_all = exchange(p_sent, "z").reshape(chips * 32, size)
    leaving = row_blocks(expert_out, experts, rows)
    returned = hand_back(leaving)
    moe_out = pl.pallas_call(
        functools.partial(combine_kernel, experts=experts, rows=rows),
        out_shape=shape_of(count, width, dtype=bf16),
        in_specs=vmem(3),
        out_specs=vmem(1)[0],
        name="combine",
    )(returned, ids, probs)
    mixed_sent, saved = pl.pallas_call(
        functools.partial(score_kernel, peers=peers),
        out_shape=(shape_of(peers, 32, size, dtype=bf16), shape_of(3, peers, 128)),
        in_specs=[HBM] + vmem(2) + [SMEM],
        out_specs=tuple(vmem(2)),
        name="score",
    )(leaving[1], q_all, near(p_all), me)
    mixed = exchange(mixed_sent, "yc")
    dq, dp_sent, loss = pl.pallas_call(
        functools.partial(coeff_kernel, peers=peers),
        out_shape=(shape_of(CHUNKS, size), shape_of(chips * 16, size, dtype=bf16), shape_of(1, 128)),
        in_specs=vmem(3) + [SMEM],
        out_specs=tuple(vmem(3)),
        name="coeff",
    )(near(mixed), saved, q_all, me)
    dp = exchange(dp_sent.reshape(chips, 2 * CHUNKS, size), "z")
    grad, grad_sent = pl.pallas_call(
        grad_kernel,
        out_shape=(shape_of(SEGS * CHUNKS, size), shape_of(experts, 8, width, dtype=bf16)),
        in_specs=vmem(4),
        out_specs=tuple(vmem(2)),
        name="text_grad",
    )(dq, near(dp), unit, inverse)
    grad_all = exchange(grad_sent, "expert").reshape(experts * 8, width)
    row_grad = pl.pallas_call(
        functools.partial(backward_kernel, experts=experts, rows=rows),
        out_shape=shape_of(slots, width, dtype=bf16),
        in_specs=vmem(5) + [HBM] * 2,
        out_specs=HBM,
        scratch_shapes=[wide, wide, outgoing, pltpu.SemaphoreType.DMA((6,))],
        name="expert_backward",
        compiler_params=LIMIT,
    )(near(grad_all), share, gate_slope, up_slope, near(down_mat), gate_mat, up_mat)
    back = exchange(row_grad.reshape(experts, rows, width), "expert").reshape(slots, width)
    gate_grad = pl.pallas_call(
        functools.partial(gate_grad_kernel, experts=experts, rows=rows),
        out_shape=shape_of(top, count),
        in_specs=vmem(3),
        out_specs=vmem(1)[0],
        name="gate_grad",
    )(returned, ids, grad)
    token_grad = pl.pallas_call(
        functools.partial(token_grad_kernel, experts=experts, rows=rows),
        out_shape=shape_of(count, width, dtype=bf16),
        in_specs=vmem(2),
        out_specs=vmem(1)[0],
        name="token_grad",
    )(near(back), ids)
    return (moe_out, token_grad, gate_grad.T, loss[:, :1])


def solution(mesh):
    dp, expert = mesh.devices.shape
    chips = Z_CHIPS if dp % Z_CHIPS == 0 else 2
    grid = Mesh(np.asarray(mesh.devices).reshape(chips, dp // chips, expert), ("z", "yc", "expert"))
    every = ("z", "yc", "expert")
    in_specs = (
        P(every, None),
        P(every, None),
        P(every, None),
        P("expert", None, None),
        P("expert", None, None),
        P("expert", None, None),
        P("expert", ("z", "yc"), None),
        P("expert", ("z", "yc"), None),
        P("expert", ("z", "yc")),
    )
    out_specs = (
        P(every, None),
        P(every, None),
        P(every, None),
        P("expert", ("z", "yc")),
    )
    return jax.shard_map(shards, mesh=grid, in_specs=in_specs, out_specs=out_specs, check_vma=False)
```

```python
import functools

import jax
import jax.numpy as jnp
import numpy as np
from jax import lax
from jax.experimental import pallas as pl
from jax.experimental.pallas import tpu as pltpu
from jax.sharding import Mesh
from jax.sharding import PartitionSpec as P

QLEN = 32
PLEN = 48
SEGS = 3
CHUNKS = 8
Z_CHIPS = 12

student_scale = 50.0
teacher_scale = 80.0
loss_scale = 64.0
norm_eps = 1e-06

f32 = jnp.float32
bf16 = jnp.bfloat16
exact = lax.Precision.HIGHEST


def iota(shape, axis):
    return lax.broadcasted_iota(jnp.int32, shape, axis)


def dot(left, right, dims=((1,), (0,)), precision=None):
    return lax.dot_general(left, right, (dims, ((), ())), precision=precision, preferred_element_type=f32)


def segment_mask(rows, count, repeat):
    token = iota((rows, count), 1)
    text = jnp.where(token < QLEN, 0, jnp.where(token < QLEN + PLEN, 1, 2))
    return (text == iota((rows, count), 0) // repeat).astype(f32)


def routing(ids):
    count = ids.shape[1]
    expert = iota((8, count), 0)
    first = expert == ids[0:1, :]
    second = expert == ids[1:2, :]
    hit = jnp.where(first, 1.0, jnp.where(second, 1.0, 0.0))
    before = (iota((count, count), 0) < iota((count, count), 1)).astype(bf16)
    rank = dot(hit.astype(bf16), before)
    return jnp.where(hit > 0.0, rank, -1.0), first, second


def slot_hits(rank, experts, rows):
    count = rank.shape[1]
    slot = iota((rows, count), 0).astype(f32)
    return [(slot == rank[e : e + 1, :]).astype(f32) for e in range(experts)]


def dispatch_kernel(tok_ref, ids_ref, prob_ref, send_hbm, send_ref, sems, *, experts, cap, rows):
    count = tok_ref.shape[0]
    rank, first, second = routing(ids_ref[...])
    probs = prob_ref[...].astype(f32)
    weight = jnp.where(first, probs[0:1, :], jnp.where(second, probs[1:2, :], 0.0))
    wide = slot_hits(rank, experts, 128)
    segs = segment_mask(8, count, 1)
    place = (iota((rows, 8), 0) == cap + iota((rows, 8), 1)).astype(bf16)
    metas = []
    for e in range(experts):
        by_text = (segs * weight[e : e + 1, :]).astype(bf16)
        meta = dot(by_text, wide[e].astype(bf16), ((1,), (1,)))
        metas.append(dot(place, meta.astype(bf16)))
    pick = jnp.concatenate([hits[:rows] for hits in wide], axis=0).astype(bf16)
    width = tok_ref.shape[1]
    step = width // 4
    metas = jnp.concatenate(metas, axis=0)
    sent = []
    for n in range(4):
        span = slice(step * n, step * (n + 1))
        block = dot(pick, tok_ref[:, span])
        if n == 0:
            block = jnp.concatenate([block[:, 0:128] + metas, block[:, 128:]], axis=1)
        send_ref[:, span] = block.astype(bf16)
        sent += fetch((send_ref.at[:, span],), (send_hbm.at[:, span],), sems, n)
    for copy in sent:
        copy.wait()


def unit_block(values):
    inverse = lax.rsqrt(jnp.sum(values * values, keepdims=True) + norm_eps)
    return values * inverse, inverse


def to_chunks(row, size):
    which = iota((CHUNKS, size), 0)
    out = jnp.zeros((CHUNKS, size), f32)
    for j in range(CHUNKS):
        out = jnp.where(which == j, row[:, j * size : (j + 1) * size], out)
    return out


def combine_kernel(ret_ref, ids_ref, prob_ref, moe_ref, *, experts, rows):
    rank, first, second = routing(ids_ref[...])
    probs = prob_ref[...].astype(f32)
    weight = jnp.where(first, probs[0:1, :], jnp.where(second, probs[1:2, :], 0.0))
    hits = slot_hits(rank, experts, rows)
    mix = jnp.concatenate([hits[e] * weight[e : e + 1, :] for e in range(experts)], axis=0).astype(bf16)
    moe_ref[...] = dot(mix, ret_ref[...], ((0,), (0,))).astype(bf16)


def teacher_kernel(_, tq_ref, tp_ref, pos_ref, out_ref):
    size = out_ref.shape[1]
    teach_p = tp_ref[...].astype(f32)
    out_ref[0:8] = unit_block(to_chunks(tq_ref[...].astype(f32), size))[0]
    out_ref[8:16] = unit_block(to_chunks(teach_p[0:1], size))[0]
    out_ref[16:24] = unit_block(to_chunks(teach_p[1:2], size))[0]
    pos = pos_ref[0, 0]
    lane = iota((8, size), 1)
    out_ref[24:32] = jnp.where(lane == 0, (pos >> 4).astype(f32), jnp.where(lane == 1, (pos & 15).astype(f32), 0.0))


def text_kernel(pool_ref, teach_ref, unit_ref, inv_ref, qs_ref, ps_ref):
    pooled = pool_ref[0]
    for e in range(1, pool_ref.shape[0]):
        pooled = pooled + pool_ref[e]
    query, query_inv = unit_block(pooled[0:8] * (1.0 / QLEN))
    pass_a, pass_a_inv = unit_block(pooled[8:16] * (1.0 / PLEN))
    pass_b, pass_b_inv = unit_block(pooled[16:24] * (1.0 / PLEN))
    unit_ref[...] = jnp.concatenate([query, pass_a, pass_b], axis=0)
    inv_ref[...] = jnp.concatenate(
        [jnp.broadcast_to(inverse, (8, 128)) for inverse in (query_inv, pass_a_inv, pass_b_inv)], axis=0
    )
    queries = jnp.concatenate([query, teach_ref[0:8], teach_ref[24:32]], axis=0).astype(bf16)
    passages = jnp.concatenate([pass_a, pass_b, teach_ref[8:24]], axis=0).astype(bf16)
    for peer in range(qs_ref.shape[0]):
        qs_ref[peer] = queries
    for peer in range(ps_ref.shape[0]):
        ps_ref[peer] = passages


def passage_of(col):
    return (col // 32) * 2 + (col % 16) // 8


def score_kernel(_, q_ref, p_ref, me_ref, sent_ref, saved_ref, score_ref, *, peers):
    q_rows = q_ref.shape[0]
    p_rows, size = p_ref.shape
    valid_count = p_rows // 16
    queries = q_ref[...]
    passages = p_ref[...]
    products = dot(queries, passages, ((1,), (1,)))
    row = iota((q_rows, 1), 0)
    col = iota((1, p_rows), 1)
    place = col % 32
    chunk = place % 8
    key = row % 24
    products = jnp.where(jnp.where(key < 16, key, -1) == jnp.where(place < 16, chunk, 8 + chunk), products, 0.0)
    products = jnp.sum(products.reshape(3 * peers, 8, p_rows), axis=1)
    join = (passage_of(iota((p_rows, 1), 0)) == iota((p_rows, 128), 1)).astype(f32)
    score_ref[...] = dot(products, join, precision=exact)
    student = student_scale * score_ref[pl.ds(0, peers, stride=3), :]
    teacher = teacher_scale * score_ref[pl.ds(1, peers, stride=3), :]
    mark_pick = (iota((peers, q_rows), 1) == 24 * iota((peers, q_rows), 0) + 16).astype(bf16)
    marks = dot(mark_pick, queries)
    pos = (16.0 * marks[:, 0:1] + marks[:, 1:2]).astype(jnp.int32)
    lane = iota((peers, 128), 1)
    number = (lane // 2) * (2 * peers) + lane % 2 + 2 * me_ref[0, 0]
    valid = lane < valid_count
    is_pos = jnp.where(valid & (number == pos), 1.0, 0.0)
    student_exp = jnp.where(valid, jnp.exp(student), 0.0)
    teacher_exp = jnp.where(valid, jnp.exp(teacher), 0.0)
    saved_ref[0] = student_exp
    saved_ref[1] = teacher_exp
    saved_ref[2] = is_pos
    parts = (student_exp, teacher_exp, teacher_exp * (teacher - student), is_pos * student)
    sums = jnp.zeros((peers, 128), f32)
    for n, part in enumerate(parts):
        rest = jnp.sum(part, axis=1, keepdims=True)
        for piece in range(3):
            head = rest.astype(bf16).astype(f32)
            sums = jnp.where(lane == 4 * piece + n, head, sums)
            rest = rest - head
    sums = jnp.concatenate([sums[0 : peers // 2], sums[peers // 2 : peers]], axis=1)
    if sums.shape[0] < 8:
        sums = jnp.concatenate([sums] + [jnp.zeros_like(sums)] * (8 // sums.shape[0] - 1), axis=0)
    sums = sums.astype(bf16)
    weights = jnp.concatenate([student_exp, teacher_exp, is_pos], axis=0).astype(bf16)
    spread = (iota((q_rows, 3 * peers), 1) == (key // 8) * peers + row // 24).astype(bf16)
    join = (iota((128, p_rows), 0) == passage_of(col)).astype(bf16)
    mixing = dot(dot(spread, weights).astype(bf16), join)
    mixing = jnp.where(row % 8 == jnp.where(place < 16, chunk, -1), mixing, 0.0).astype(bf16)
    mixed = dot(mixing, passages)
    for peer in range(peers):
        sent_ref[peer, 0:24, :] = mixed[24 * peer : 24 * peer + 24].astype(bf16)
        sent_ref[peer, 24:32, :] = sums


def coeff_kernel(got_ref, saved_ref, q_ref, me_ref, dq_ref, dp_ref, loss_ref, *, peers):
    q_rows = q_ref.shape[0]
    rows = dp_ref.shape[0]
    total = got_ref[0].astype(f32)
    for peer in range(1, peers):
        total = total + got_ref[peer].astype(f32)
    half = peers // 2

    def quantity(n):
        cols = []
        for side in (0, 128):
            at = side + n
            block = total[24 : 24 + half]
            cols.append(block[:, at : at + 1] + block[:, at + 4 : at + 5] + block[:, at + 8 : at + 9])
        return jnp.concatenate(cols, axis=0)

    student_total, teacher_total, cross, positive = quantity(0), quantity(1), quantity(2), quantity(3)
    loss = 2.0 * jnp.log(student_total) - positive + cross / teacher_total - jnp.log(teacher_total)
    mine = iota((peers, 1), 0) == me_ref[0, 0]
    own = lambda values: jnp.sum(jnp.where(mine, values, 0.0), keepdims=True)
    loss_ref[...] = jnp.broadcast_to(own(loss), (1, 128))
    dq_ref[...] = student_scale * (
        total[0:8] * (2.0 / own(student_total)) - total[8:16] / own(teacher_total) - total[16:24]
    )
    coeffs = (2.0 * saved_ref[0] / student_total - saved_ref[1] / teacher_total - saved_ref[2]).astype(bf16)
    row = iota((rows, 1), 0)
    col = iota((1, q_rows), 1)
    key = col % 24
    spread = (row // CHUNKS == iota((rows, 128), 1)).astype(bf16)
    join = (iota((peers, q_rows), 0) == col // 24).astype(bf16)
    by_passage = dot(dot(spread, coeffs, ((1,), (1,))).astype(bf16), join)
    by_passage = jnp.where(row % 8 == jnp.where(key < 8, key, -1), by_passage, 0.0).astype(bf16)
    dp_ref[...] = (student_scale * dot(by_passage, q_ref[...])).astype(bf16)


def grad_kernel(dq_ref, dp_ref, unit_ref, inv_ref, grad_ref, sent_ref):
    passage = dp_ref[0].astype(f32)
    for peer in range(1, dp_ref.shape[0]):
        passage = passage + dp_ref[peer].astype(f32)
    parts = []
    for s, (unit_grad, scale) in enumerate(
        ((dq_ref[...], loss_scale / QLEN), (passage[0:8], loss_scale / PLEN), (passage[8:16], loss_scale / PLEN))
    ):
        unit = unit_ref[8 * s : 8 * s + 8, :]
        inverse = inv_ref[8 * s : 8 * s + 8, 0:1]
        along = jnp.sum(unit * unit_grad, keepdims=True)
        parts.append(scale * (inverse * (unit_grad - unit * along)))
    grad = jnp.concatenate(parts, axis=0)
    grad_ref[...] = grad
    high = grad.astype(bf16).astype(f32)
    split = jnp.concatenate([high, grad - high], axis=0).astype(bf16)
    texts, size = grad.shape
    row = iota((8, 2 * texts), 0)
    first = row // SEGS * texts + row % SEGS * CHUNKS
    for j in range(CHUNKS):
        pick = ((iota((8, 2 * texts), 1) == first + j) & (row < 2 * SEGS)).astype(bf16)
        rows = dot(pick, split).astype(bf16)
        for peer in range(sent_ref.shape[0]):
            sent_ref[peer, :, size * j : size * (j + 1)] = rows


def fetch(sources, targets, sems, base):
    copies = [pltpu.make_async_copy(a, b, sems.at[base + n]) for n, (a, b) in enumerate(zip(sources, targets))]
    for copy in copies:
        copy.start()
    return copies


def forward_kernel(
    x_ref,
    gate_ref,
    up_hbm,
    down_hbm,
    hidden_hbm,
    pool_ref,
    gate_slope_hbm,
    up_slope_hbm,
    share_ref,
    up_ref,
    down_ref,
    hidden_ref,
    gate_slope_ref,
    up_slope_ref,
    sems,
    *,
    experts,
    at,
):
    width = down_ref.shape[1]
    size = width // CHUNKS
    half = width // 2
    top = (up_hbm.at[0:half], up_ref.at[0:half])
    low = (up_hbm.at[half:], up_ref.at[half:])
    copies = fetch((top[0], low[0], down_hbm), (top[1], low[1], down_ref), sems, 0)
    slots = x_ref.shape[0]
    rows = slots // experts
    row = iota((8, 128), 0)
    lane = iota((8, 128), 1)
    wanted = (row >= at) & (row < at + SEGS) & (lane < rows)
    pick_row = iota((8, 8), 0)
    pick = ((iota((8, 8), 1) == at + pick_row % SEGS) & (pick_row < 2 * SEGS)).astype(bf16)
    shares = []
    for s in range(experts):
        share = jnp.where(wanted, x_ref[rows * (s + 1) - 8 : rows * (s + 1), 0:128].astype(f32), 0.0)
        share = dot(pick, share.astype(bf16))
        share_ref[s] = share
        shares.append(share[:, 0:rows].astype(bf16))
    pre_gate = dot(x_ref[...], gate_ref[...])
    sigmoid = jax.nn.sigmoid(pre_gate)
    active = pre_gate * sigmoid
    slope = sigmoid * (1.0 + pre_gate * (1.0 - sigmoid))
    up_slope_ref[...] = active.astype(bf16)
    copies[0].wait()
    pre_up = dot(x_ref[:, 0:half], up_ref[0:half])
    copies[1].wait()
    pre_up = pre_up + dot(x_ref[:, half:], up_ref[half:])
    gate_slope_ref[...] = (pre_up * slope).astype(bf16)
    hidden = active * pre_up
    hidden_ref[...] = hidden.astype(bf16)
    sent = fetch(
        (hidden_ref, up_slope_ref, gate_slope_ref), (hidden_hbm, up_slope_hbm, gate_slope_hbm), sems, 3
    )
    text = jnp.concatenate(
        [dot(shares[s], hidden[rows * s : rows * (s + 1)].astype(bf16)) for s in range(experts)], axis=0
    )
    high = text.astype(bf16).astype(f32)
    stacked = jnp.concatenate([high, text - high], axis=0).astype(bf16)
    copies[2].wait()
    part = dot(stacked, down_ref[...])
    text = part[0 : 8 * experts] + part[8 * experts :]
    for s in range(experts):
        for t in range(SEGS):
            one = 8 * s + t
            pool_ref[s, 8 * t : 8 * t + 8, :] = to_chunks(text[one : one + 1], size)
    for copy in sent:
        copy.wait()


def down_kernel(hidden_ref, down_ref, out_ref):
    out_ref[...] = dot(hidden_ref[...], down_ref[...]).astype(bf16)


def backward_kernel(
    grad_ref,
    share_ref,
    gate_slope_ref,
    up_slope_ref,
    down_ref,
    gate_hbm,
    up_hbm,
    out_hbm,
    gate_ref,
    up_ref,
    out_ref,
    sems,
    *,
    experts,
    rows,
):
    width = gate_ref.shape[0]
    half = width // 2
    parts = [(hbm.at[half * n : half * (n + 1)], ref.at[half * n : half * (n + 1)])
             for n in range(2) for hbm, ref in ((gate_hbm, gate_ref), (up_hbm, up_ref))]
    copies = fetch([part[0] for part in parts], [part[1] for part in parts], sems, 0)
    by_text = dot(grad_ref[...], down_ref[...], ((1,), (1,)))
    high = by_text.astype(bf16).astype(f32)
    low = by_text - high
    blocks = []
    for s in range(experts):
        share = jnp.concatenate([share_ref[s], share_ref[s]], axis=0).astype(bf16)
        split = jnp.concatenate([high[8 * s : 8 * s + 8], low[8 * s : 8 * s + 8]], axis=0).astype(bf16)
        blocks.append(dot(share, split, ((0,), (0,)))[:rows])
    hidden_grad = jnp.concatenate(blocks, axis=0)
    gate_part = (hidden_grad * gate_slope_ref[...].astype(f32)).astype(bf16)
    up_part = (hidden_grad * up_slope_ref[...].astype(f32)).astype(bf16)
    sent = []
    for n in range(2):
        span = slice(half * n, half * (n + 1))
        copies[2 * n].wait()
        part = dot(gate_part, gate_ref[span], ((1,), (1,)))
        copies[2 * n + 1].wait()
        out_ref[:, span] = (part + dot(up_part, up_ref[span], ((1,), (1,)))).astype(bf16)
        sent += fetch((out_ref.at[:, span],), (out_hbm.at[:, span],), sems, 4 + n)
    for copy in sent:
        copy.wait()


def gate_grad_kernel(ret_ref, ids_ref, grad_ref, out_ref, pick_ref, *, experts, rows):
    count = ids_ref.shape[1]
    size = ret_ref.shape[1] // CHUNKS
    slots = ret_ref.shape[0]
    rank, first, second = routing(ids_ref[...])
    grad = grad_ref[...]
    high = grad.astype(bf16)
    low = (grad - high.astype(f32)).astype(bf16)
    both = jnp.concatenate([high.astype(f32), low.astype(f32)], axis=0).astype(bf16)
    n = 2 * SEGS * CHUNKS
    chunk = iota((n, slots), 0) % CHUNKS
    acc = jnp.zeros((n, slots), f32)
    for j in range(CHUNKS):
        part = dot(both, ret_ref[:, j * size : (j + 1) * size], ((1,), (1,)))
        acc = jnp.where(chunk == j, part, acc)
    gather = (iota((8, n), 1) // CHUNKS % SEGS == iota((8, n), 0)).astype(f32)
    by_slot = dot(gather, acc, precision=exact)
    hits = slot_hits(rank, experts, rows)
    same = (iota((count, count), 0) == iota((count, count), 1)).astype(bf16)
    pick_ref[...] = dot(same, jnp.concatenate(hits, axis=0).astype(bf16), ((1,), (1,))).astype(bf16)
    texts = segment_mask(8, count, 1)
    results = []
    for named in (first, second):
        named = jnp.where(named, 1.0, 0.0)
        pick = jnp.concatenate([hits[e] * named[e : e + 1, :] for e in range(experts)], axis=0)
        results.append(jnp.sum(texts * dot(by_slot, pick, precision=exact), axis=0, keepdims=True))
    out_ref[...] = jnp.where(iota((2, count), 0) == 0, results[0], results[1])


def token_grad_kernel(back_ref, pick_ref, out_ref):
    out_ref[...] = dot(pick_ref[...], back_ref[...]).astype(bf16)


LIMIT = pltpu.CompilerParams(vmem_limit_bytes=52 * 1024 * 1024)


def near(values):
    return pltpu.with_memory_space_constraint(values, pltpu.VMEM)


def vmem(count):
    return [pl.BlockSpec(memory_space=pltpu.VMEM)] * count


HBM = pl.BlockSpec(memory_space=pltpu.HBM)
SMEM = pl.BlockSpec(memory_space=pltpu.SMEM)


def shape_of(*dims, dtype=f32):
    return jax.ShapeDtypeStruct(dims, dtype)


def row_blocks(values, experts, rows):
    me = lax.axis_index("expert")
    blocks = values.reshape(experts, rows, values.shape[1])
    take = lambda n: lax.dynamic_index_in_dim(blocks, n % experts, 0, keepdims=False)
    return [take(me + step) for step in range(experts)]


def hand_back(leaving):
    me = lax.axis_index("expert")
    experts = len(leaving)
    out = jnp.zeros((experts,) + leaving[0].shape, leaving[0].dtype)
    for step in range(experts):
        pairs = [(n, (n + step) % experts) for n in range(experts)]
        got = lax.ppermute(leaving[step], "expert", pairs) if step else leaving[0]
        out = lax.dynamic_update_slice(out, got[None], ((me - step) % experts, 0, 0))
    return out.reshape(-1, out.shape[2])


def exchange(values, axis):
    return lax.all_to_all(values, axis, split_axis=0, concat_axis=0, tiled=True)


def shards(
    tokens,
    expert_ids,
    gate_probs,
    w_gate,
    w_up,
    w_down,
    teacher_queries,
    teacher_passages,
    positives,
):
    experts = lax.axis_size("expert")
    peers = lax.axis_size("yc")
    chips = lax.axis_size("z")
    count, width = tokens.shape
    size = width // CHUNKS
    top = expert_ids.shape[1]
    cap = min(count, (count * top * 33 + 32 * experts - 1) // (32 * experts))
    rows = (cap + SEGS + 7) // 8 * 8
    slots = experts * rows
    ids = expert_ids.T
    probs = gate_probs.T
    me = lax.axis_index("yc").astype(jnp.int32).reshape(1, 1)
    gate_mat = w_gate[0]
    up_mat = w_up[0]
    down_mat = w_down[0]

    sent = pl.pallas_call(
        functools.partial(dispatch_kernel, experts=experts, cap=cap, rows=rows),
        out_shape=shape_of(slots, width, dtype=bf16),
        in_specs=vmem(3),
        out_specs=HBM,
        scratch_shapes=[pltpu.VMEM((slots, width), bf16), pltpu.SemaphoreType.DMA((4,))],
        name="dispatch",
    )(tokens, ids, probs)
    teach = pl.pallas_call(
        teacher_kernel,
        out_shape=shape_of(32, size),
        in_specs=[HBM] + vmem(2) + [SMEM],
        out_specs=vmem(1)[0],
        name="teacher",
    )(sent, teacher_queries[0], teacher_passages[0], positives)
    arrived = exchange(sent.reshape(experts, rows, width), "expert")
    hidden_size = gate_mat.shape[1]
    wide = pltpu.VMEM((width, hidden_size), bf16)
    tall = pltpu.VMEM((hidden_size, width), bf16)
    slope = pltpu.VMEM((slots, hidden_size), bf16)
    outgoing = pltpu.VMEM((slots, width), bf16)
    hidden, pool_sent, gate_slope, up_slope, share = pl.pallas_call(
        functools.partial(forward_kernel, experts=experts, at=cap - (rows - 8)),
        out_shape=(
            shape_of(slots, hidden_size, dtype=bf16),
            shape_of(experts, SEGS * CHUNKS, size),
            shape_of(slots, hidden_size, dtype=bf16),
            shape_of(slots, hidden_size, dtype=bf16),
            shape_of(experts, 8, 128),
        ),
        in_specs=vmem(2) + [HBM] * 2,
        out_specs=(HBM, vmem(1)[0], HBM, HBM, vmem(1)[0]),
        scratch_shapes=[wide, tall, slope, slope, slope, pltpu.SemaphoreType.DMA((6,))],
        name="expert_forward",
        compiler_params=LIMIT,
    )(arrived.reshape(slots, width), near(gate_mat), up_mat, down_mat)
    expert_out = pl.pallas_call(
        down_kernel,
        out_shape=shape_of(slots, width, dtype=bf16),
        in_specs=vmem(2),
        out_specs=vmem(1)[0],
        name="expert_down",
    )(hidden, down_mat)
    pool = exchange(pool_sent, "expert")
    unit, inverse, q_sent, p_sent = pl.pallas_call(
        text_kernel,
        out_shape=(
            shape_of(SEGS * CHUNKS, size),
            shape_of(SEGS * CHUNKS, 128),
            shape_of(peers, 24, size, dtype=bf16),
            shape_of(chips, 32, size, dtype=bf16),
        ),
        in_specs=vmem(2),
        out_specs=tuple(vmem(4)),
        name="text",
    )(near(pool), teach)
    with jax.named_scope("q_gather"):
        q_all = exchange(q_sent, "yc").reshape(peers * 24, size)
    with jax.named_scope("p_gather"):
        p_all = exchange(p_sent, "z").reshape(chips * 32, size)
    leaving = row_blocks(expert_out, experts, rows)
    returned = hand_back(leaving)
    moe_out = pl.pallas_call(
        functools.partial(combine_kernel, experts=experts, rows=rows),
        out_shape=shape_of(count, width, dtype=bf16),
        in_specs=vmem(3),
        out_specs=vmem(1)[0],
        name="combine",
    )(returned, ids, probs)
    mixed_sent, saved = pl.pallas_call(
        functools.partial(score_kernel, peers=peers),
        out_shape=(shape_of(peers, 32, size, dtype=bf16), shape_of(3, peers, 128)),
        in_specs=[HBM] + vmem(2) + [SMEM],
        out_specs=tuple(vmem(2)),
        scratch_shapes=[pltpu.VMEM((3 * peers, 128), f32)],
        name="score",
    )(leaving[1], q_all, near(p_all), me)
    mixed = exchange(mixed_sent, "yc")
    dq, dp_sent, loss = pl.pallas_call(
        functools.partial(coeff_kernel, peers=peers),
        out_shape=(shape_of(CHUNKS, size), shape_of(chips * 16, size, dtype=bf16), shape_of(1, 128)),
        in_specs=vmem(3) + [SMEM],
        out_specs=tuple(vmem(3)),
        name="coeff",
    )(near(mixed), saved, q_all, me)
    dp = exchange(dp_sent.reshape(chips, 2 * CHUNKS, size), "z")
    grad, grad_sent = pl.pallas_call(
        grad_kernel,
        out_shape=(shape_of(SEGS * CHUNKS, size), shape_of(experts, 8, width, dtype=bf16)),
        in_specs=vmem(4),
        out_specs=tuple(vmem(2)),
        name="text_grad",
    )(dq, near(dp), unit, inverse)
    grad_all = exchange(grad_sent, "expert").reshape(experts * 8, width)
    row_grad = pl.pallas_call(
        functools.partial(backward_kernel, experts=experts, rows=rows),
        out_shape=shape_of(slots, width, dtype=bf16),
        in_specs=vmem(5) + [HBM] * 2,
        out_specs=HBM,
        scratch_shapes=[wide, wide, outgoing, pltpu.SemaphoreType.DMA((6,))],
        name="expert_backward",
        compiler_params=LIMIT,
    )(near(grad_all), share, gate_slope, up_slope, near(down_mat), gate_mat, up_mat)
    back = exchange(row_grad.reshape(experts, rows, width), "expert").reshape(slots, width)
    gate_grad, pick = pl.pallas_call(
        functools.partial(gate_grad_kernel, experts=experts, rows=rows),
        out_shape=(shape_of(top, count), shape_of(count, slots, dtype=bf16)),
        in_specs=vmem(3),
        out_specs=tuple(vmem(2)),
        name="gate_grad",
    )(returned, ids, grad)
    token_grad = pl.pallas_call(
        token_grad_kernel,
        out_shape=shape_of(count, width, dtype=bf16),
        in_specs=vmem(2),
        out_specs=vmem(1)[0],
        name="token_grad",
    )(near(back), pick)
    return (moe_out, token_grad, gate_grad.T, loss[:, :1])


def solution(mesh):
    dp, expert = mesh.devices.shape
    chips = Z_CHIPS if dp % Z_CHIPS == 0 else 2
    grid = Mesh(np.asarray(mesh.devices).reshape(chips, dp // chips, expert), ("z", "yc", "expert"))
    every = ("z", "yc", "expert")
    in_specs = (
        P(every, None),
        P(every, None),
        P(every, None),
        P("expert", None, None),
        P("expert", None, None),
        P("expert", None, None),
        P("expert", ("z", "yc"), None),
        P("expert", ("z", "yc"), None),
        P("expert", ("z", "yc")),
    )
    out_specs = (
        P(every, None),
        P(every, None),
        P(every, None),
        P("expert", ("z", "yc")),
    )
    return jax.shard_map(shards, mesh=grid, in_specs=in_specs, out_specs=out_specs, check_vma=False)
```

```python
import functools

import jax
import jax.numpy as jnp
import numpy as np
from jax import lax
from jax.experimental import pallas as pl
from jax.experimental.pallas import tpu as pltpu
from jax.sharding import Mesh
from jax.sharding import PartitionSpec as P

QLEN = 32
PLEN = 48
SEGS = 3
CHUNKS = 8
Z_CHIPS = 12

student_scale = 50.0
teacher_scale = 80.0
loss_scale = 64.0
norm_eps = 1e-06

f32 = jnp.float32
bf16 = jnp.bfloat16
exact = lax.Precision.HIGHEST


def iota(shape, axis):
    return lax.broadcasted_iota(jnp.int32, shape, axis)


def dot(left, right, dims=((1,), (0,)), precision=None):
    return lax.dot_general(left, right, (dims, ((), ())), precision=precision, preferred_element_type=f32)


def segment_mask(rows, count, repeat):
    token = iota((rows, count), 1)
    text = jnp.where(token < QLEN, 0, jnp.where(token < QLEN + PLEN, 1, 2))
    return (text == iota((rows, count), 0) // repeat).astype(f32)


def routing(ids):
    count = ids.shape[1]
    expert = iota((8, count), 0)
    first = expert == ids[0:1, :]
    second = expert == ids[1:2, :]
    hit = jnp.where(first, 1.0, jnp.where(second, 1.0, 0.0))
    before = (iota((count, count), 0) < iota((count, count), 1)).astype(bf16)
    rank = dot(hit.astype(bf16), before)
    return jnp.where(hit > 0.0, rank, -1.0), first, second


def slot_hits(rank, experts, rows):
    count = rank.shape[1]
    slot = iota((rows, count), 0).astype(f32)
    return [(slot == rank[e : e + 1, :]).astype(f32) for e in range(experts)]


def dispatch_kernel(tok_ref, ids_ref, prob_ref, send_hbm, send_ref, sems, *, experts, cap, rows):
    count = tok_ref.shape[0]
    rank, first, second = routing(ids_ref[...])
    probs = prob_ref[...].astype(f32)
    weight = jnp.where(first, probs[0:1, :], jnp.where(second, probs[1:2, :], 0.0))
    wide = slot_hits(rank, experts, 128)
    segs = segment_mask(8, count, 1)
    place = (iota((rows, 8), 0) == cap + iota((rows, 8), 1)).astype(bf16)
    metas = []
    for e in range(experts):
        by_text = (segs * weight[e : e + 1, :]).astype(bf16)
        meta = dot(by_text, wide[e].astype(bf16), ((1,), (1,)))
        metas.append(dot(place, meta.astype(bf16)))
    pick = jnp.concatenate([hits[:rows] for hits in wide], axis=0).astype(bf16)
    width = tok_ref.shape[1]
    step = width // 4
    metas = jnp.concatenate(metas, axis=0)
    sent = []
    for n in range(4):
        span = slice(step * n, step * (n + 1))
        block = dot(pick, tok_ref[:, span])
        if n == 0:
            block = jnp.concatenate([block[:, 0:128] + metas, block[:, 128:]], axis=1)
        send_ref[:, span] = block.astype(bf16)
        sent += fetch((send_ref.at[:, span],), (send_hbm.at[:, span],), sems, n)
    for copy in sent:
        copy.wait()


def unit_block(values):
    inverse = lax.rsqrt(jnp.sum(values * values, keepdims=True) + norm_eps)
    return values * inverse, inverse


def to_chunks(row, size):
    which = iota((CHUNKS, size), 0)
    out = jnp.zeros((CHUNKS, size), f32)
    for j in range(CHUNKS):
        out = jnp.where(which == j, row[:, j * size : (j + 1) * size], out)
    return out


def combine_kernel(ret_ref, ids_ref, prob_ref, moe_ref, *, experts, rows):
    rank, first, second = routing(ids_ref[...])
    probs = prob_ref[...].astype(f32)
    weight = jnp.where(first, probs[0:1, :], jnp.where(second, probs[1:2, :], 0.0))
    hits = slot_hits(rank, experts, rows)
    mix = jnp.concatenate([hits[e] * weight[e : e + 1, :] for e in range(experts)], axis=0).astype(bf16)
    moe_ref[...] = dot(mix, ret_ref[...], ((0,), (0,))).astype(bf16)


def teacher_kernel(_, tq_ref, tp_ref, pos_ref, out_ref):
    size = out_ref.shape[1]
    teach_p = tp_ref[...].astype(f32)
    out_ref[0:8] = unit_block(to_chunks(tq_ref[...].astype(f32), size))[0]
    out_ref[8:16] = unit_block(to_chunks(teach_p[0:1], size))[0]
    out_ref[16:24] = unit_block(to_chunks(teach_p[1:2], size))[0]
    pos = pos_ref[0, 0]
    lane = iota((8, size), 1)
    out_ref[24:32] = jnp.where(lane == 0, (pos >> 4).astype(f32), jnp.where(lane == 1, (pos & 15).astype(f32), 0.0))


def text_kernel(pool_ref, teach_ref, unit_ref, inv_ref, qs_ref, ps_ref):
    pooled = pool_ref[0]
    for e in range(1, pool_ref.shape[0]):
        pooled = pooled + pool_ref[e]
    query, query_inv = unit_block(pooled[0:8] * (1.0 / QLEN))
    pass_a, pass_a_inv = unit_block(pooled[8:16] * (1.0 / PLEN))
    pass_b, pass_b_inv = unit_block(pooled[16:24] * (1.0 / PLEN))
    unit_ref[...] = jnp.concatenate([query, pass_a, pass_b], axis=0)
    inv_ref[...] = jnp.concatenate(
        [jnp.broadcast_to(inverse, (8, 128)) for inverse in (query_inv, pass_a_inv, pass_b_inv)], axis=0
    )
    queries = jnp.concatenate([query, teach_ref[0:8], teach_ref[24:32]], axis=0).astype(bf16)
    passages = jnp.concatenate([pass_a, pass_b, teach_ref[8:24]], axis=0).astype(bf16)
    for peer in range(qs_ref.shape[0]):
        qs_ref[peer] = queries
    for peer in range(ps_ref.shape[0]):
        ps_ref[peer] = passages


def passage_of(col):
    return (col // 32) * 2 + (col % 16) // 8


def score_kernel(_, q_ref, p_ref, me_ref, sent_ref, saved_ref, score_ref, *, peers):
    q_rows = q_ref.shape[0]
    p_rows, size = p_ref.shape
    valid_count = p_rows // 16
    queries = q_ref[...]
    passages = p_ref[...]
    products = dot(queries, passages, ((1,), (1,)))
    row = iota((q_rows, 1), 0)
    col = iota((1, p_rows), 1)
    place = col % 32
    chunk = place % 8
    key = row % 24
    products = jnp.where(jnp.where(key < 16, key, -1) == jnp.where(place < 16, chunk, 8 + chunk), products, 0.0)
    products = jnp.sum(products.reshape(3 * peers, 8, p_rows), axis=1)
    join = (passage_of(iota((p_rows, 1), 0)) == iota((p_rows, 128), 1)).astype(f32)
    score_ref[...] = dot(products, join, precision=exact)
    student = student_scale * score_ref[pl.ds(0, peers, stride=3), :]
    teacher = teacher_scale * score_ref[pl.ds(1, peers, stride=3), :]
    mark_pick = (iota((peers, q_rows), 1) == 24 * iota((peers, q_rows), 0) + 16).astype(bf16)
    marks = dot(mark_pick, queries)
    pos = (16.0 * marks[:, 0:1] + marks[:, 1:2]).astype(jnp.int32)
    lane = iota((peers, 128), 1)
    number = (lane // 2) * (2 * peers) + lane % 2 + 2 * me_ref[0, 0]
    valid = lane < valid_count
    is_pos = jnp.where(valid & (number == pos), 1.0, 0.0)
    student_exp = jnp.where(valid, jnp.exp(student), 0.0)
    teacher_exp = jnp.where(valid, jnp.exp(teacher), 0.0)
    saved_ref[0] = student_exp
    saved_ref[1] = teacher_exp
    saved_ref[2] = is_pos
    parts = (student_exp, teacher_exp, teacher_exp * (teacher - student), is_pos * student)
    sums = jnp.zeros((peers, 128), f32)
    for n, part in enumerate(parts):
        rest = jnp.sum(part, axis=1, keepdims=True)
        for piece in range(3):
            head = rest.astype(bf16).astype(f32)
            sums = jnp.where(lane == 4 * piece + n, head, sums)
            rest = rest - head
    sums = jnp.concatenate([sums[0 : peers // 2], sums[peers // 2 : peers]], axis=1)
    if sums.shape[0] < 8:
        sums = jnp.concatenate([sums] + [jnp.zeros_like(sums)] * (8 // sums.shape[0] - 1), axis=0)
    sums = sums.astype(bf16)
    weights = jnp.concatenate([student_exp, teacher_exp, is_pos], axis=0).astype(bf16)
    spread = (iota((q_rows, 3 * peers), 1) == (key // 8) * peers + row // 24).astype(bf16)
    join = (iota((128, p_rows), 0) == passage_of(col)).astype(bf16)
    mixing = dot(dot(spread, weights).astype(bf16), join)
    mixing = jnp.where(row % 8 == jnp.where(place < 16, chunk, -1), mixing, 0.0).astype(bf16)
    mixed = dot(mixing, passages)
    for peer in range(peers):
        sent_ref[peer, 0:24, :] = mixed[24 * peer : 24 * peer + 24].astype(bf16)
        sent_ref[peer, 24:32, :] = sums


def coeff_kernel(got_ref, saved_ref, q_ref, me_ref, dq_ref, dp_ref, loss_ref, *, peers):
    q_rows = q_ref.shape[0]
    rows = dp_ref.shape[0]
    total = got_ref[0].astype(f32)
    for peer in range(1, peers):
        total = total + got_ref[peer].astype(f32)
    half = peers // 2

    def quantity(n):
        cols = []
        for side in (0, 128):
            at = side + n
            block = total[24 : 24 + half]
            cols.append(block[:, at : at + 1] + block[:, at + 4 : at + 5] + block[:, at + 8 : at + 9])
        return jnp.concatenate(cols, axis=0)

    student_total, teacher_total, cross, positive = quantity(0), quantity(1), quantity(2), quantity(3)
    loss = 2.0 * jnp.log(student_total) - positive + cross / teacher_total - jnp.log(teacher_total)
    mine = iota((peers, 1), 0) == me_ref[0, 0]
    own = lambda values: jnp.sum(jnp.where(mine, values, 0.0), keepdims=True)
    loss_ref[...] = jnp.broadcast_to(own(loss), (1, 128))
    dq_ref[...] = student_scale * (
        total[0:8] * (2.0 / own(student_total)) - total[8:16] / own(teacher_total) - total[16:24]
    )
    coeffs = (2.0 * saved_ref[0] / student_total - saved_ref[1] / teacher_total - saved_ref[2]).astype(bf16)
    row = iota((rows, 1), 0)
    col = iota((1, q_rows), 1)
    key = col % 24
    spread = (row // CHUNKS == iota((rows, 128), 1)).astype(bf16)
    join = (iota((peers, q_rows), 0) == col // 24).astype(bf16)
    by_passage = dot(dot(spread, coeffs, ((1,), (1,))).astype(bf16), join)
    by_passage = jnp.where(row % 8 == jnp.where(key < 8, key, -1), by_passage, 0.0).astype(bf16)
    dp_ref[...] = (student_scale * dot(by_passage, q_ref[...])).astype(bf16)


def grad_kernel(dq_ref, dp_ref, unit_ref, inv_ref, grad_ref, sent_ref):
    passage = dp_ref[0].astype(f32)
    for peer in range(1, dp_ref.shape[0]):
        passage = passage + dp_ref[peer].astype(f32)
    parts = []
    for s, (unit_grad, scale) in enumerate(
        ((dq_ref[...], loss_scale / QLEN), (passage[0:8], loss_scale / PLEN), (passage[8:16], loss_scale / PLEN))
    ):
        unit = unit_ref[8 * s : 8 * s + 8, :]
        inverse = inv_ref[8 * s : 8 * s + 8, 0:1]
        along = jnp.sum(unit * unit_grad, keepdims=True)
        parts.append(scale * (inverse * (unit_grad - unit * along)))
    grad = jnp.concatenate(parts, axis=0)
    grad_ref[...] = grad
    high = grad.astype(bf16).astype(f32)
    split = jnp.concatenate([high, grad - high], axis=0).astype(bf16)
    texts, size = grad.shape
    row = iota((8, 2 * texts), 0)
    first = row // SEGS * texts + row % SEGS * CHUNKS
    for j in range(CHUNKS):
        pick = ((iota((8, 2 * texts), 1) == first + j) & (row < 2 * SEGS)).astype(bf16)
        rows = dot(pick, split).astype(bf16)
        for peer in range(sent_ref.shape[0]):
            sent_ref[peer, :, size * j : size * (j + 1)] = rows


def fetch(sources, targets, sems, base):
    copies = [pltpu.make_async_copy(a, b, sems.at[base + n]) for n, (a, b) in enumerate(zip(sources, targets))]
    for copy in copies:
        copy.start()
    return copies


def forward_kernel(
    x_ref,
    gate_ref,
    up_hbm,
    down_hbm,
    hidden_hbm,
    pool_ref,
    gate_slope_hbm,
    up_slope_hbm,
    share_ref,
    up_ref,
    down_ref,
    hidden_ref,
    gate_slope_ref,
    up_slope_ref,
    sems,
    *,
    experts,
    at,
):
    width = down_ref.shape[1]
    size = width // CHUNKS
    half = width // 2
    top = (up_hbm.at[0:half], up_ref.at[0:half])
    low = (up_hbm.at[half:], up_ref.at[half:])
    copies = fetch((top[0], low[0], down_hbm), (top[1], low[1], down_ref), sems, 0)
    slots = x_ref.shape[0]
    rows = slots // experts
    row = iota((8, 128), 0)
    lane = iota((8, 128), 1)
    wanted = (row >= at) & (row < at + SEGS) & (lane < rows)
    pick_row = iota((8, 8), 0)
    pick = ((iota((8, 8), 1) == at + pick_row % SEGS) & (pick_row < 2 * SEGS)).astype(bf16)
    shares = []
    for s in range(experts):
        share = jnp.where(wanted, x_ref[rows * (s + 1) - 8 : rows * (s + 1), 0:128].astype(f32), 0.0)
        share = dot(pick, share.astype(bf16))
        share_ref[s] = share
        shares.append(share[:, 0:rows].astype(bf16))
    pre_gate = dot(x_ref[...], gate_ref[...])
    sigmoid = jax.nn.sigmoid(pre_gate)
    active = pre_gate * sigmoid
    slope = sigmoid * (1.0 + pre_gate * (1.0 - sigmoid))
    up_slope_ref[...] = active.astype(bf16)
    copies[0].wait()
    pre_up = dot(x_ref[:, 0:half], up_ref[0:half])
    copies[1].wait()
    pre_up = pre_up + dot(x_ref[:, half:], up_ref[half:])
    gate_slope_ref[...] = (pre_up * slope).astype(bf16)
    hidden = active * pre_up
    hidden_ref[...] = hidden.astype(bf16)
    sent = fetch(
        (hidden_ref, up_slope_ref, gate_slope_ref), (hidden_hbm, up_slope_hbm, gate_slope_hbm), sems, 3
    )
    text = jnp.concatenate(
        [dot(shares[s], hidden[rows * s : rows * (s + 1)].astype(bf16)) for s in range(experts)], axis=0
    )
    high = text.astype(bf16).astype(f32)
    stacked = jnp.concatenate([high, text - high], axis=0).astype(bf16)
    copies[2].wait()
    part = dot(stacked, down_ref[...])
    text = part[0 : 8 * experts] + part[8 * experts :]
    for s in range(experts):
        for t in range(SEGS):
            one = 8 * s + t
            pool_ref[s, 8 * t : 8 * t + 8, :] = to_chunks(text[one : one + 1], size)
    for copy in sent:
        copy.wait()


def down_kernel(hidden_ref, down_ref, out_ref):
    out_ref[...] = dot(hidden_ref[...], down_ref[...]).astype(bf16)


def backward_kernel(
    grad_ref,
    share_ref,
    gate_slope_ref,
    up_slope_ref,
    down_ref,
    gate_hbm,
    up_hbm,
    out_hbm,
    gate_ref,
    up_ref,
    out_ref,
    sems,
    *,
    experts,
    rows,
):
    width = gate_ref.shape[0]
    half = width // 2
    parts = [(hbm.at[half * n : half * (n + 1)], ref.at[half * n : half * (n + 1)])
             for n in range(2) for hbm, ref in ((gate_hbm, gate_ref), (up_hbm, up_ref))]
    copies = fetch([part[0] for part in parts], [part[1] for part in parts], sems, 0)
    by_text = dot(grad_ref[...], down_ref[...], ((1,), (1,)))
    high = by_text.astype(bf16).astype(f32)
    low = by_text - high
    blocks = []
    for s in range(experts):
        share = jnp.concatenate([share_ref[s], share_ref[s]], axis=0).astype(bf16)
        split = jnp.concatenate([high[8 * s : 8 * s + 8], low[8 * s : 8 * s + 8]], axis=0).astype(bf16)
        blocks.append(dot(share, split, ((0,), (0,)))[:rows])
    hidden_grad = jnp.concatenate(blocks, axis=0)
    gate_part = (hidden_grad * gate_slope_ref[...].astype(f32)).astype(bf16)
    up_part = (hidden_grad * up_slope_ref[...].astype(f32)).astype(bf16)
    sent = []
    for n in range(2):
        span = slice(half * n, half * (n + 1))
        copies[2 * n].wait()
        part = dot(gate_part, gate_ref[span], ((1,), (1,)))
        copies[2 * n + 1].wait()
        out_ref[:, span] = (part + dot(up_part, up_ref[span], ((1,), (1,)))).astype(bf16)
        sent += fetch((out_ref.at[:, span],), (out_hbm.at[:, span],), sems, 4 + n)
    for copy in sent:
        copy.wait()


def gate_grad_kernel(ret_ref, ids_ref, grad_ref, out_ref, pick_ref, *, experts, rows):
    count = ids_ref.shape[1]
    size = ret_ref.shape[1] // CHUNKS
    slots = ret_ref.shape[0]
    rank, first, second = routing(ids_ref[...])
    grad = grad_ref[...]
    high = grad.astype(bf16)
    low = (grad - high.astype(f32)).astype(bf16)
    both = jnp.concatenate([high.astype(f32), low.astype(f32)], axis=0).astype(bf16)
    n = 2 * SEGS * CHUNKS
    chunk = iota((n, slots), 0) % CHUNKS
    acc = jnp.zeros((n, slots), f32)
    for j in range(CHUNKS):
        part = dot(both, ret_ref[:, j * size : (j + 1) * size], ((1,), (1,)))
        acc = jnp.where(chunk == j, part, acc)
    gather = (iota((8, n), 1) // CHUNKS % SEGS == iota((8, n), 0)).astype(f32)
    by_slot = dot(gather, acc, precision=exact)
    hits = slot_hits(rank, experts, rows)
    same = (iota((count, count), 0) == iota((count, count), 1)).astype(bf16)
    pick_ref[...] = dot(same, jnp.concatenate(hits, axis=0).astype(bf16), ((1,), (1,))).astype(bf16)
    texts = segment_mask(8, count, 1)
    results = []
    for named in (first, second):
        named = jnp.where(named, 1.0, 0.0)
        pick = jnp.concatenate([hits[e] * named[e : e + 1, :] for e in range(experts)], axis=0)
        results.append(jnp.sum(texts * dot(by_slot, pick, precision=exact), axis=0, keepdims=True))
    out_ref[...] = jnp.where(iota((2, count), 0) == 0, results[0], results[1])


LIMIT = pltpu.CompilerParams(vmem_limit_bytes=52 * 1024 * 1024)


def near(values):
    return pltpu.with_memory_space_constraint(values, pltpu.VMEM)


def vmem(count):
    return [pl.BlockSpec(memory_space=pltpu.VMEM)] * count


HBM = pl.BlockSpec(memory_space=pltpu.HBM)
SMEM = pl.BlockSpec(memory_space=pltpu.SMEM)


def shape_of(*dims, dtype=f32):
    return jax.ShapeDtypeStruct(dims, dtype)


def row_blocks(values, experts, rows):
    me = lax.axis_index("expert")
    blocks = values.reshape(experts, rows, values.shape[1])
    take = lambda n: lax.dynamic_index_in_dim(blocks, n % experts, 0, keepdims=False)
    return [take(me + step) for step in range(experts)]


def hand_back(leaving):
    me = lax.axis_index("expert")
    experts = len(leaving)
    out = jnp.zeros((experts,) + leaving[0].shape, leaving[0].dtype)
    for step in range(experts):
        pairs = [(n, (n + step) % experts) for n in range(experts)]
        got = lax.ppermute(leaving[step], "expert", pairs) if step else leaving[0]
        out = lax.dynamic_update_slice(out, got[None], ((me - step) % experts, 0, 0))
    return out.reshape(-1, out.shape[2])


def exchange(values, axis):
    return lax.all_to_all(values, axis, split_axis=0, concat_axis=0, tiled=True)


def shards(
    tokens,
    expert_ids,
    gate_probs,
    w_gate,
    w_up,
    w_down,
    teacher_queries,
    teacher_passages,
    positives,
):
    experts = lax.axis_size("expert")
    peers = lax.axis_size("yc")
    chips = lax.axis_size("z")
    count, width = tokens.shape
    size = width // CHUNKS
    top = expert_ids.shape[1]
    cap = min(count, (count * top * 33 + 32 * experts - 1) // (32 * experts))
    rows = (cap + SEGS + 7) // 8 * 8
    slots = experts * rows
    ids = expert_ids.T
    probs = gate_probs.T
    me = lax.axis_index("yc").astype(jnp.int32).reshape(1, 1)
    gate_mat = w_gate[0]
    up_mat = w_up[0]
    down_mat = w_down[0]

    sent = pl.pallas_call(
        functools.partial(dispatch_kernel, experts=experts, cap=cap, rows=rows),
        out_shape=shape_of(slots, width, dtype=bf16),
        in_specs=vmem(3),
        out_specs=HBM,
        scratch_shapes=[pltpu.VMEM((slots, width), bf16), pltpu.SemaphoreType.DMA((4,))],
        name="dispatch",
    )(tokens, ids, probs)
    teach = pl.pallas_call(
        teacher_kernel,
        out_shape=shape_of(32, size),
        in_specs=[HBM] + vmem(2) + [SMEM],
        out_specs=vmem(1)[0],
        name="teacher",
    )(sent, teacher_queries[0], teacher_passages[0], positives)
    arrived = exchange(sent.reshape(experts, rows, width), "expert")
    hidden_size = gate_mat.shape[1]
    wide = pltpu.VMEM((width, hidden_size), bf16)
    tall = pltpu.VMEM((hidden_size, width), bf16)
    slope = pltpu.VMEM((slots, hidden_size), bf16)
    outgoing = pltpu.VMEM((slots, width), bf16)
    hidden, pool_sent, gate_slope, up_slope, share = pl.pallas_call(
        functools.partial(forward_kernel, experts=experts, at=cap - (rows - 8)),
        out_shape=(
            shape_of(slots, hidden_size, dtype=bf16),
            shape_of(experts, SEGS * CHUNKS, size),
            shape_of(slots, hidden_size, dtype=bf16),
            shape_of(slots, hidden_size, dtype=bf16),
            shape_of(experts, 8, 128),
        ),
        in_specs=vmem(2) + [HBM] * 2,
        out_specs=(HBM, vmem(1)[0], HBM, HBM, vmem(1)[0]),
        scratch_shapes=[wide, tall, slope, slope, slope, pltpu.SemaphoreType.DMA((6,))],
        name="expert_forward",
        compiler_params=LIMIT,
    )(arrived.reshape(slots, width), near(gate_mat), up_mat, down_mat)
    expert_out = pl.pallas_call(
        down_kernel,
        out_shape=shape_of(slots, width, dtype=bf16),
        in_specs=vmem(2),
        out_specs=vmem(1)[0],
        name="expert_down",
    )(hidden, down_mat)
    pool = exchange(pool_sent, "expert")
    unit, inverse, q_sent, p_sent = pl.pallas_call(
        text_kernel,
        out_shape=(
            shape_of(SEGS * CHUNKS, size),
            shape_of(SEGS * CHUNKS, 128),
            shape_of(peers, 24, size, dtype=bf16),
            shape_of(chips, 32, size, dtype=bf16),
        ),
        in_specs=vmem(2),
        out_specs=tuple(vmem(4)),
        name="text",
    )(near(pool), teach)
    with jax.named_scope("q_gather"):
        q_all = exchange(q_sent, "yc").reshape(peers * 24, size)
    with jax.named_scope("p_gather"):
        p_all = exchange(p_sent, "z").reshape(chips * 32, size)
    leaving = row_blocks(expert_out, experts, rows)
    returned = hand_back(leaving)
    moe_out = pl.pallas_call(
        functools.partial(combine_kernel, experts=experts, rows=rows),
        out_shape=shape_of(count, width, dtype=bf16),
        in_specs=vmem(3),
        out_specs=vmem(1)[0],
        name="combine",
    )(returned, ids, probs)
    mixed_sent, saved = pl.pallas_call(
        functools.partial(score_kernel, peers=peers),
        out_shape=(shape_of(peers, 32, size, dtype=bf16), shape_of(3, peers, 128)),
        in_specs=[HBM] + vmem(2) + [SMEM],
        out_specs=tuple(vmem(2)),
        scratch_shapes=[pltpu.VMEM((3 * peers, 128), f32)],
        name="score",
    )(leaving[1], q_all, near(p_all), me)
    mixed = exchange(mixed_sent, "yc")
    dq, dp_sent, loss = pl.pallas_call(
        functools.partial(coeff_kernel, peers=peers),
        out_shape=(shape_of(CHUNKS, size), shape_of(chips * 16, size, dtype=bf16), shape_of(1, 128)),
        in_specs=vmem(3) + [SMEM],
        out_specs=tuple(vmem(3)),
        name="coeff",
    )(near(mixed), saved, q_all, me)
    dp = exchange(dp_sent.reshape(chips, 2 * CHUNKS, size), "z")
    grad, grad_sent = pl.pallas_call(
        grad_kernel,
        out_shape=(shape_of(SEGS * CHUNKS, size), shape_of(experts, 8, width, dtype=bf16)),
        in_specs=vmem(4),
        out_specs=tuple(vmem(2)),
        name="text_grad",
    )(dq, near(dp), unit, inverse)
    grad_all = exchange(grad_sent, "expert").reshape(experts * 8, width)
    row_grad = pl.pallas_call(
        functools.partial(backward_kernel, experts=experts, rows=rows),
        out_shape=shape_of(slots, width, dtype=bf16),
        in_specs=vmem(5) + [HBM] * 2,
        out_specs=HBM,
        scratch_shapes=[wide, wide, outgoing, pltpu.SemaphoreType.DMA((6,))],
        name="expert_backward",
        compiler_params=LIMIT,
    )(near(grad_all), share, gate_slope, up_slope, near(down_mat), gate_mat, up_mat)
    back = exchange(row_grad.reshape(experts, rows, width), "expert").reshape(slots, width)
    gate_grad, pick = pl.pallas_call(
        functools.partial(gate_grad_kernel, experts=experts, rows=rows),
        out_shape=(shape_of(top, count), shape_of(count, slots, dtype=bf16)),
        in_specs=vmem(3),
        out_specs=tuple(vmem(2)),
        name="gate_grad",
    )(returned, ids, grad)
    token_grad = dot(pick, back).astype(bf16)
    return (moe_out, token_grad, gate_grad.T, loss[:, :1])


def solution(mesh):
    dp, expert = mesh.devices.shape
    chips = Z_CHIPS if dp % Z_CHIPS == 0 else 2
    grid = Mesh(np.asarray(mesh.devices).reshape(chips, dp // chips, expert), ("z", "yc", "expert"))
    every = ("z", "yc", "expert")
    in_specs = (
        P(every, None),
        P(every, None),
        P(every, None),
        P("expert", None, None),
        P("expert", None, None),
        P("expert", None, None),
        P("expert", ("z", "yc"), None),
        P("expert", ("z", "yc"), None),
        P("expert", ("z", "yc")),
    )
    out_specs = (
        P(every, None),
        P(every, None),
        P(every, None),
        P("expert", ("z", "yc")),
    )
    return jax.shard_map(shards, mesh=grid, in_specs=in_specs, out_specs=out_specs, check_vma=False)
```
